32 devices in a mesh: lat: 8 (over y, x, core), lon: 4 (over z).
Axes of the slice: x: 2, y: 2, z: 4, core: 2. Of those that a mesh axis runs over, the one named last changes fastest.
Arguments:
- tracer: float32 [16, 64, 2880], P(None, 'lat', 'lon'), may hold values from -6 to 6
- zonal_courant: float32 [16, 64, 2880], P(None, 'lat', 'lon'), may hold values from -0.35 to 0.35
- north_courant: float32 [16, 64, 2880], P(None, 'lat', 'lon'), may hold values from -0.35 to 0.35
- cutoff: int32 [16], replicated, may hold values from 1 to 128
Outputs:
- advanced: float32 [16, 64, 2880], P(None, 'lat', 'lon')
The draws below stay inside these ranges and needn't reach their ends.
All inputs are finite; a program needn't handle non-finite values.
Results may differ from the reference program's by a relative error of at most 0.0001.
Values sent between devices are 32-bit elements; how exact they have to be, the bound alone decides.
A program may use at most 64 MiB of HBM per device.

```python
import jax
import jax.numpy as jnp

NLON = 2880
KMAX = 128
LEV = 16
NLAT = 64
CAP_ROWS = 8


def set_ends(values, key, low, high):
    index_at = [jax.random.randint(jax.random.fold_in(key, axis), (), 0, length) for axis, length in enumerate(values.shape)]
    main_axis = values.shape.index(max(values.shape))
    beside = index_at[:main_axis] + [(index_at[main_axis] + 1) % values.shape[main_axis]] + index_at[main_axis + 1:]
    return values.at[tuple(index_at)].set(low).at[tuple(beside)].set(high)


def levels(stream_key, extent, cuts, low, largest):
    def one(dim, blocks):
        steps = jax.random.uniform(jax.random.fold_in(jax.random.fold_in(stream_key, 6), dim), (blocks,), jnp.float32, low / len(cuts), largest / len(cuts))
        return jnp.repeat(jnp.exp(steps), extent[dim] // blocks).reshape((-1,) + (1,) * (len(extent) - dim - 1))

    loudness = one(*cuts[0])
    for cut in cuts[1:]:
        loudness = loudness * one(*cut)
    return loudness


def centred(own_key, shape, deviation, bound, shards=(), held_as=jnp.bfloat16):
    gain = levels(own_key, shape, shards, -0.22, 0.18) if shards else 1.0
    drawn = jax.random.normal(own_key, shape, jnp.float32) * deviation * gain
    return jnp.minimum(jnp.maximum(drawn, -bound), bound).astype(held_as)


def setup_inputs(seed: int = 0) -> dict:
    key_of = jax.random.split(jax.random.key(seed), 5)
    return {
        "tracer": centred(key_of[0], (LEV, NLAT, NLON), 1.0, 6.0, ((1, 8), (2, 4)), jnp.float32),
        "zonal_courant": jnp.clip(jax.random.uniform(key_of[1], (LEV, NLAT, NLON), jnp.float32, -0.35, 0.35) * levels(key_of[1], (LEV, NLAT, NLON), ((1, 8), (2, 4)), -0.4, 0.0), -0.35, 0.35),
        "north_courant": jnp.clip(jax.random.uniform(key_of[2], (LEV, NLAT, NLON), jnp.float32, -0.35, 0.35) * levels(key_of[2], (LEV, NLAT, NLON), ((1, 8), (2, 4)), -0.4, 0.0), -0.35, 0.35),
        "cutoff": set_ends(jax.random.randint(key_of[3], (2 * CAP_ROWS,), 1, KMAX + 1), jax.random.fold_in(key_of[3], 1), 1, KMAX).astype(jnp.int32),
    }


DIFFUSION = 0.2


def tendency_of(tracer, zonal_courant, north_courant):
    half_turn = NLON // 2
    south_edge = jnp.roll(tracer[:, :1], half_turn, axis=2)
    north_edge = jnp.roll(tracer[:, -1:], half_turn, axis=2)
    padded = jnp.concatenate([south_edge, tracer, north_edge], axis=1)
    south_cell = padded[:, :-2]
    north_cell = padded[:, 2:]
    east_cell = jnp.roll(tracer, -1, axis=2)
    west_cell = jnp.roll(tracer, 1, axis=2)
    return (-0.5 * zonal_courant * (east_cell - west_cell)
            - 0.5 * north_courant * (north_cell - south_cell)
            + DIFFUSION * (east_cell + west_cell + north_cell + south_cell - 4.0 * tracer))


def polar_filter(rows_block, cut_rows):
    spectrum = jnp.fft.rfft(rows_block, axis=-1)
    modes = jnp.arange(spectrum.shape[-1], dtype=jnp.int32)
    kept_modes = modes[None, None, :] < cut_rows[None, :, None]
    spectrum = jnp.where(kept_modes, spectrum, jnp.zeros_like(spectrum))
    return jnp.fft.irfft(spectrum, n=NLON, axis=-1).astype(jnp.float32)


def reference(tracer, zonal_courant, north_courant, cutoff):
    cap_rows = CAP_ROWS
    state = tracer
    for substep in range(2):
        tendency = tendency_of(state, zonal_courant, north_courant)
        south_part = polar_filter(tendency[:, :cap_rows], cutoff[:cap_rows])
        north_part = polar_filter(tendency[:, -cap_rows:], cutoff[cap_rows:])
        tendency = jnp.concatenate([south_part, tendency[:, cap_rows:-cap_rows], north_part], axis=1)
        state = state + tendency
    return state
```

```python
import functools
import math

import jax
import jax.numpy as jnp
import numpy as np
from jax import lax
from jax.experimental import pallas as pl
from jax.experimental.pallas import tpu as pltpu
from jax.sharding import PartitionSpec as P

KMAX = 128
DIFFUSION = 0.2
LANES = 128
MESH = pl.DeviceIdType.MESH
F32 = jnp.float32
BF16 = jnp.bfloat16


def split_table(table):
    high = table.astype(np.float32).astype(BF16)
    low = (table - high.astype(np.float64)).astype(np.float32).astype(BF16)
    return np.stack([high, low])


def trig(columns, total):
    modes = np.arange(KMAX)
    angle = (columns[:, None] * modes[None, :] % total) * (2.0 * math.pi / total)
    return np.concatenate([np.cos(angle), np.sin(angle)], axis=1)


def window_basis(cols, total):
    bandwidth = (KMAX - 0.5) / total
    place = np.arange(cols)
    operator = np.diag(((cols - 1 - 2 * place) / 2.0) ** 2 * math.cos(2.0 * math.pi * bandwidth))
    beside = np.arange(1, cols) * (cols - np.arange(1, cols)) / 2.0
    operator = operator + np.diag(beside, 1) + np.diag(beside, -1)
    vectors = np.linalg.eigh(operator)[1][:, ::-1]
    half = vectors[:(cols + 1) // 2]
    peak = np.take_along_axis(half, np.abs(half).argmax(0)[None], 0)[0]
    return vectors * np.where(peak < 0, -1.0, 1.0)


def tables(cols, width, lon_count):
    total = cols * lon_count
    kept = min(LANES, cols)
    basis = np.zeros((width, LANES))
    basis[:cols, :kept] = window_basis(cols, total)[:, :kept]
    analysis = np.concatenate(list(split_table(basis)), axis=1)
    expand = np.zeros((lon_count, LANES, 2 * KMAX))
    for step in range(lon_count):
        expand[step] = basis[:cols].T @ trig(np.arange(cols) + step * cols, total)
    expand = split_table(expand.reshape(lon_count * LANES, 2 * KMAX))
    lane = np.arange(width)
    lane = np.where(lane == width - 1, -1, lane)
    synthesis = split_table(trig(lane, total).T.copy())
    ends = np.zeros((lon_count, 8, 2 * KMAX), np.float32)
    ends[:, 0] = trig(np.arange(lon_count) * cols, total)
    ends[:, 1] = trig(np.arange(lon_count) * cols + cols - 1, total)
    return analysis, expand, synthesis, ends


def split(value):
    high = value.astype(BF16)
    low = (value - high.astype(F32)).astype(BF16)
    return high, low


def dot3(value, table):
    high, low = split(value)
    t_high = table[0]
    t_low = table[1]
    dot = functools.partial(jnp.dot, preferred_element_type=F32)
    return dot(high, t_high) + (dot(low, t_high) + dot(high, t_low))


def dot_pair(value, table):
    size = value.shape[0]
    both = jnp.dot(jnp.concatenate(split(value), axis=0), table[...], preferred_element_type=F32)
    return both[:size, :LANES] + (both[:size, LANES:] + both[size:, :LANES])


def kernel(
    lat_count, lon_count, cap_blocks,
    cut_ref, tracer, zonal, north, ana_hbm, exp_hbm, syn_hbm, ends_hbm, out,
    q_in, zc, nc, ana, exp, syn, ends, q, tend,
    row_first, row_second, col_out, col_in, part, extra,
    load_sem, row_send, row_recv, col_send, col_recv, sum_send, sum_recv,
):
    rows, levels, cols = q_in.shape
    width = q.shape[2]
    total = cols * lon_count
    lat = lax.axis_index("lat")
    lon = lax.axis_index("lon")
    polar = jnp.logical_or(lat < cap_blocks, lat >= lat_count - cap_blocks)
    first = lat == 0
    last = lat == lat_count - 1
    east = lax.rem(lon + 1, lon_count)
    west = lax.rem(lon + lon_count - 1, lon_count)
    across = lax.rem(lon + lon_count // 2, lon_count)
    peers = [lax.rem(lon + step, lon_count) for step in range(lon_count)]
    steps = range(1, lon_count)
    order = [0, rows - 1, 1, rows - 2] + list(range(2, rows - 2))
    pieces = (((2, rows), (0, 2)), ((4, rows), (0, 4)))

    loads = []
    for index, (source, target) in enumerate(((tracer, q_in), (zonal, zc), (north, nc))):
        for row in range(rows):
            loads.append(pltpu.make_async_copy(
                source.at[:, row, :], target.at[row], load_sem.at[index * rows + row]))
    for load in loads[:rows]:
        load.start()

    barrier = pltpu.get_barrier_semaphore()

    def greet(there):
        pl.semaphore_signal(barrier, inc=1, device_id=there, device_id_type=MESH)

    @pl.when(jnp.logical_not(first))
    def _():
        greet({"lat": lat - 1, "lon": lon})

    @pl.when(jnp.logical_not(last))
    def _():
        greet({"lat": lat + 1, "lon": lon})

    @pl.when(polar)
    def _():
        for step in steps:
            greet({"lat": lat, "lon": peers[step]})

    @pl.when(jnp.logical_not(polar))
    def _():
        greet({"lat": lat, "lon": east})
        greet({"lat": lat, "lon": west})

    for load in loads[rows:]:
        load.start()
    tables_in = [
        pltpu.make_async_copy(ana_hbm, ana, load_sem.at[3 * rows]),
        pltpu.make_async_copy(exp_hbm, exp, load_sem.at[3 * rows + 1]),
        pltpu.make_async_copy(syn_hbm, syn, load_sem.at[3 * rows + 2]),
        pltpu.make_async_copy(ends_hbm, ends, load_sem.at[3 * rows + 3]),
    ]
    for load in tables_in:
        load.start()

    edge = first.astype(jnp.int32) + last.astype(jnp.int32)
    sides = jnp.where(polar, lon_count - 1, 2)
    pl.semaphore_wait(barrier, 2 - edge + sides)

    def row_copy(turn, slot, row, there):
        source = tracer.at[:, row, :] if turn == 0 else q.at[row]
        target = row_first if turn == 0 else row_second
        return pltpu.make_async_remote_copy(
            source, target.at[slot],
            row_send.at[turn, 0 if row else 1], row_recv.at[turn, slot],
            device_id=there, device_id_type=MESH)

    def to_north(turn):
        return row_copy(turn, 0, rows - 1, {"lat": lat + 1, "lon": lon})

    def to_south(turn):
        return row_copy(turn, 1, 0, {"lat": lat - 1, "lon": lon})

    def over_north():
        return row_copy(0, 1, rows - 1, {"lat": lat, "lon": across})

    def over_south():
        return row_copy(0, 0, 0, {"lat": lat, "lon": across})

    @pl.when(last)
    def _():
        over_north().start()

    @pl.when(first)
    def _():
        over_south().start()

    @pl.when(jnp.logical_not(last))
    def _():
        to_north(0).start()

    @pl.when(jnp.logical_not(first))
    def _():
        to_south(0).start()

    def rows_arrive(turn):
        @pl.when(jnp.logical_not(last))
        def _():
            to_south(turn).wait_recv()
            to_north(turn).wait_send()

        @pl.when(jnp.logical_not(first))
        def _():
            to_north(turn).wait_recv()
            to_south(turn).wait_send()

    def poles_arrive():
        @pl.when(last)
        def _():
            over_north().wait()

        @pl.when(first)
        def _():
            over_south().wait()

    lane = lax.broadcasted_iota(jnp.int32, (levels, LANES), 1)
    end_tile = (cols - 1) // LANES * LANES
    end_lane = (cols - 1) % LANES
    east_tile = cols // LANES * LANES
    west_tile = width - LANES

    def pack_cols(turn):
        packed = jnp.zeros((levels, LANES), F32)

        def put(packed, at, tile, came_from):
            return jnp.where(lane == at, pltpu.roll(tile, (at - came_from) % LANES, 1), packed)

        for row in range(rows):
            packed = put(packed, row, q[row, :, end_tile:end_tile + LANES], end_lane)
            packed = put(packed, rows + row, q[row, :, 0:LANES], 0)
        return packed

    def pack_factors(packed):
        for row in range(rows):
            tile = zc[row, :, end_tile:cols]
            if cols - end_tile < LANES:
                tile = jnp.concatenate(
                    [tile, jnp.zeros((levels, LANES - cols + end_tile), F32)], axis=1)
            factor = DIFFUSION - 0.5 * tile
            packed = jnp.where(
                lane == 2 * rows + row,
                pltpu.roll(factor, (2 * rows + row - end_lane) % LANES, 1), packed)
            factor = DIFFUSION + 0.5 * zc[row, :, 0:LANES]
            packed = jnp.where(
                lane == 3 * rows + row, pltpu.roll(factor, 3 * rows + row, 1), packed)
        return packed

    def place_cols(turn):
        from_west = col_in[turn, lon_count - 1]
        from_east = col_in[turn, 1]
        for row in range(rows):
            tile = q[row, :, east_tile:east_tile + LANES]
            moved = pltpu.roll(from_east, (cols % LANES - rows - row) % LANES, 1)
            q[row, :, east_tile:east_tile + LANES] = jnp.where(lane == cols % LANES, moved, tile)
            tile = q[row, :, west_tile:west_tile + LANES]
            moved = pltpu.roll(from_west, (LANES - 1 - row) % LANES, 1)
            q[row, :, west_tile:west_tile + LANES] = jnp.where(lane == LANES - 1, moved, tile)

    def col_copy(turn, step):
        return pltpu.make_async_remote_copy(
            col_out.at[turn], col_in.at[turn, lon_count - step],
            col_send.at[turn, step], col_recv.at[turn, lon_count - step],
            device_id={"lat": lat, "lon": peers[step]}, device_id_type=MESH)

    def col_arrival(turn, step):
        theirs = col_in.at[turn, step]
        return pltpu.make_async_remote_copy(
            theirs, theirs, col_send.at[turn, step], col_recv.at[turn, step],
            device_id={"lat": lat, "lon": peers[step]}, device_id_type=MESH)

    def sum_copy(turn, piece, step):
        low, high = pieces[turn][piece]
        return pltpu.make_async_remote_copy(
            part.at[turn, 0, low:high], part.at[turn, lon_count - step, low:high],
            sum_send.at[turn, piece, step], sum_recv.at[turn, piece, lon_count - step],
            device_id={"lat": lat, "lon": peers[step]}, device_id_type=MESH)

    def sum_arrival(turn, piece, step):
        low, high = pieces[turn][piece]
        theirs = part.at[turn, step, low:high]
        return pltpu.make_async_remote_copy(
            theirs, theirs, sum_send.at[turn, piece, step], sum_recv.at[turn, piece, step],
            device_id={"lat": lat, "lon": peers[step]}, device_id_type=MESH)

    def farthest_first(send):
        for distance in range(lon_count - 1, 0, -1):
            @pl.when(lon + distance < lon_count)
            def _():
                send(distance)

            @pl.when(lon - distance >= 0)
            def _():
                send(lon_count - distance)

    def stencil(turn, row):
        beyond = row_first if turn == 0 else row_second
        here = q[row]
        to_east = pltpu.roll(here, width - 1, 1)[:, :cols]
        to_west = pltpu.roll(here, 1, 1)[:, :cols]
        here = here[:, :cols]
        up = q[row + 1, :, :cols] if row < rows - 1 else beyond[1, :, :cols]
        down = q[row - 1, :, :cols] if row else beyond[0, :, :cols]
        return (-0.5 * zc[row] * (to_east - to_west)
                - 0.5 * nc[row] * (up - down)
                + DIFFUSION * (to_east + to_west + up + down - 4.0 * here))

    q[:, :, (width - LANES):] = jnp.zeros((rows, levels, LANES), F32)
    for load in loads[:rows]:
        load.wait()
    for row in range(rows):
        q[row, :, :cols] = q_in[row]

    @pl.when(jnp.logical_not(polar))
    def _():
        col_out[0] = pack_cols(0)
        for side in (1, lon_count - 1):
            col_copy(0, side).start()
        for load in loads[rows:] + tables_in:
            load.wait()
        for side in (1, lon_count - 1):
            col_arrival(0, side).wait_recv()
        place_cols(0)
        rows_arrive(0)
        for row in range(rows):
            tend[row, :, :cols] = stencil(0, row)
        for row in range(rows):
            q[row, :, :cols] = q[row, :, :cols] + tend[row, :, :cols]
        to_north(1).start()
        to_south(1).start()
        col_out[1] = pack_cols(1)
        for side in (1, lon_count - 1):
            col_copy(1, side).start()
        for side in (1, lon_count - 1):
            col_arrival(1, side).wait_recv()
        rows_arrive(1)
        place_cols(1)
        for row in range(rows):
            out[:, row, :] = q[row, :, :cols] + stencil(1, row)
        for turn in range(2):
            for side in (1, lon_count - 1):
                col_copy(turn, side).wait_send()

    @pl.when(polar)
    def _():
        tend[:, :, (width - LANES):] = jnp.zeros((rows, levels, LANES), F32)
        for load in loads[rows:2 * rows]:
            load.wait()
        col_out[0] = pack_factors(pack_cols(0))
        farthest_first(lambda step: col_copy(0, step).start())
        for load in loads[2 * rows:] + tables_in:
            load.wait()

        offset = jnp.where(
            lat < cap_blocks, lat * rows, (lat - lat_count + 2 * cap_blocks) * rows)
        mode = lax.broadcasted_iota(jnp.int32, (1, 2 * KMAX), 1) % KMAX
        weight = jnp.where(mode == 0, 1.0 / total, 2.0 / total).astype(F32)
        keep = [jnp.where(mode < cut_ref[offset + row], weight, 0.0) for row in range(rows)]
        parity = 1.0 - 2.0 * (lax.broadcasted_iota(jnp.int32, (1, 2 * KMAX), 1) % 2).astype(F32)

        def analyse(turn, piece):
            low, high = pieces[turn][piece]
            count = high - low
            for slot in range(low, high):
                tend[slot, :, :cols] = stencil(turn, order[slot])
            found = dot_pair(tend[low:high].reshape(count * levels, width), ana)
            part[turn, 0, low:high] = found.reshape(count, levels, LANES)
            farthest_first(lambda step: sum_copy(turn, piece, step).start())

        def collect(turn, piece):
            low, high = pieces[turn][piece]
            for step in steps:
                sum_arrival(turn, piece, step).wait_recv()
            count = high - low
            gathered = jnp.concatenate(
                [part[turn, step, low:high].reshape(count * levels, LANES)
                 for step in range(lon_count)], axis=1)
            summed = dot3(gathered, exp).reshape(count, levels, 2 * KMAX)
            result = []
            for slot in range(low, high):
                total_sum = summed[slot - low]
                if turn == 0:
                    total_sum = total_sum + extra[slot]
                result.append(total_sum * keep[order[slot]])
            return result

        def synthesise(parts):
            return dot3(jnp.concatenate(parts, axis=0), syn).reshape(len(parts), levels, width)

        analyse(0, 0)
        rows_arrive(0)
        poles_arrive()
        analyse(0, 1)

        for step in steps:
            col_arrival(0, step).wait_recv()
        col_in[0, 0] = col_out[0]
        place_cols(0)
        packed = [col_in[0, step] for step in range(lon_count)]
        added = [jnp.zeros((levels, 2 * KMAX), F32) for _ in range(rows)]
        for step in range(lon_count):
            behind = packed[step - 1]
            ahead = packed[(step + 1) % lon_count]
            at_last = packed[step] * pltpu.roll(ahead, rows, 1)
            at_first = packed[step] * pltpu.roll(behind, 3 * rows, 1)
            for row in range(rows):
                column = at_last[:, 2 * rows + row:2 * rows + row + 1]
                added[row] = added[row] + column * ends[step, 1:2, :]
                column = at_first[:, 3 * rows + row:3 * rows + row + 1]
                added[row] = added[row] + column * ends[step, 0:1, :]
        for slot in range(rows):
            extra[slot] = added[order[slot]]

        low, high = pieces[0][0]
        filtered = synthesise(collect(0, 0))
        for slot in range(low, high):
            q[order[slot]] = q[order[slot]] + filtered[slot - low]
        analyse(1, 0)

        local = collect(0, 1)
        pole_row = jnp.where(first, local[0], local[1]) * parity
        filtered = synthesise(local + [pole_row])
        q[0] = q[0] + filtered[0]
        q[rows - 1] = q[rows - 1] + filtered[1]

        @pl.when(jnp.logical_not(last))
        def _():
            to_north(1).start()

        @pl.when(jnp.logical_not(first))
        def _():
            to_south(1).start()

        @pl.when(last)
        def _():
            row_second[1, :, :cols] = row_first[1] + filtered[2, :, :cols]

        @pl.when(first)
        def _():
            row_second[0, :, :cols] = row_first[0] + filtered[2, :, :cols]

        rows_arrive(1)
        analyse(1, 1)
        for piece in range(2):
            low, high = pieces[1][piece]
            filtered = synthesise(collect(1, piece))
            for slot in range(low, high):
                row = order[slot]
                out[:, row, :] = q[row, :, :cols] + filtered[slot - low, :, :cols]
        for step in steps:
            col_copy(0, step).wait_send()
            for turn in range(2):
                for piece in range(2):
                    sum_copy(turn, piece, step).wait_send()


def shards(tracer, zonal_courant, north_courant, cutoff):
    levels, rows, cols = tracer.shape
    lat_count = lax.axis_size("lat")
    lon_count = lax.axis_size("lon")
    cap_blocks = lat_count // 8
    width = -(-(cols + 2) // LANES) * LANES
    analysis, expand, synthesis, ends = tables(cols, width, lon_count)
    dma = pltpu.SemaphoreType.DMA
    anywhere = pl.BlockSpec(memory_space=pl.ANY)
    return pl.pallas_call(
        functools.partial(kernel, lat_count, lon_count, cap_blocks),
        out_shape=pltpu.VMEM(tracer.shape, F32),
        in_specs=[pl.BlockSpec(memory_space=pltpu.SMEM)] + [anywhere] * 7,
        out_specs=pl.BlockSpec(memory_space=pltpu.VMEM),
        scratch_shapes=[
            pltpu.VMEM((rows, levels, cols), F32),
            pltpu.VMEM((rows, levels, cols), F32),
            pltpu.VMEM((rows, levels, cols), F32),
            pltpu.VMEM(analysis.shape, BF16),
            pltpu.VMEM(expand.shape, BF16),
            pltpu.VMEM(synthesis.shape, BF16),
            pltpu.VMEM(ends.shape, F32),
            pltpu.VMEM((rows, levels, width), F32),
            pltpu.VMEM((rows, levels, width), F32),
            pltpu.VMEM((2, levels, cols), F32),
            pltpu.VMEM((2, levels, width), F32),
            pltpu.VMEM((2, levels, LANES), F32),
            pltpu.VMEM((2, lon_count, levels, LANES), F32),
            pltpu.VMEM((2, lon_count, rows, levels, LANES), F32),
            pltpu.VMEM((rows, levels, 2 * KMAX), F32),
            dma((3 * rows + 4,)),
            dma((2, 2)), dma((2, 2)), dma((2, lon_count)), dma((2, lon_count)),
            dma((2, 2, lon_count)), dma((2, 2, lon_count)),
        ],
        compiler_params=pltpu.CompilerParams(collective_id=0, has_side_effects=True),
    )(cutoff, tracer, zonal_courant, north_courant,
      jnp.asarray(analysis), jnp.asarray(expand), jnp.asarray(synthesis), jnp.asarray(ends))


def solution(mesh):
    return jax.shard_map(
        shards,
        mesh=mesh,
        in_specs=(P(None, "lat", "lon"), P(None, "lat", "lon"), P(None, "lat", "lon"), P()),
        out_specs=P(None, "lat", "lon"),
        check_vma=False,
    )
```

```python
import functools
import math

import jax
import jax.numpy as jnp
import numpy as np
from jax import lax
from jax.experimental import pallas as pl
from jax.experimental.pallas import tpu as pltpu
from jax.sharding import PartitionSpec as P

KMAX = 128
DIFFUSION = 0.2
LANES = 128
MESH = pl.DeviceIdType.MESH
F32 = jnp.float32
BF16 = jnp.bfloat16


def split_table(table):
    high = table.astype(np.float32).astype(BF16)
    low = (table - high.astype(np.float64)).astype(np.float32).astype(BF16)
    return np.stack([high, low])


def trig(columns, total):
    modes = np.arange(KMAX)
    angle = (columns[:, None] * modes[None, :] % total) * (2.0 * math.pi / total)
    return np.concatenate([np.cos(angle), np.sin(angle)], axis=1)


def window_basis(cols, total):
    bandwidth = (KMAX - 0.5) / total
    place = np.arange(cols)
    operator = np.diag(((cols - 1 - 2 * place) / 2.0) ** 2 * math.cos(2.0 * math.pi * bandwidth))
    beside = np.arange(1, cols) * (cols - np.arange(1, cols)) / 2.0
    operator = operator + np.diag(beside, 1) + np.diag(beside, -1)
    vectors = np.linalg.eigh(operator)[1][:, ::-1]
    half = vectors[:(cols + 1) // 2]
    peak = np.take_along_axis(half, np.abs(half).argmax(0)[None], 0)[0]
    return vectors * np.where(peak < 0, -1.0, 1.0)


def tables(cols, width, lon_count):
    total = cols * lon_count
    kept = min(LANES, cols)
    basis = np.zeros((width, LANES))
    basis[:cols, :kept] = window_basis(cols, total)[:, :kept]
    analysis = np.concatenate(list(split_table(basis)), axis=1)
    expand = np.zeros((lon_count, LANES, 2 * KMAX))
    for step in range(lon_count):
        expand[step] = basis[:cols].T @ trig(np.arange(cols) + step * cols, total)
    expand = split_table(expand.reshape(lon_count * LANES, 2 * KMAX))
    lane = np.arange(width)
    lane = np.where(lane == width - 1, -1, lane)
    synthesis = split_table(trig(lane, total).T.copy())
    ends = np.zeros((lon_count, 8, 2 * KMAX), np.float32)
    ends[:, 0] = trig(np.arange(lon_count) * cols, total)
    ends[:, 1] = trig(np.arange(lon_count) * cols + cols - 1, total)
    return analysis, expand, synthesis, ends


def split(value):
    high = value.astype(BF16)
    low = (value - high.astype(F32)).astype(BF16)
    return high, low


def dot3(value, table):
    high, low = split(value)
    t_high = table[0]
    t_low = table[1]
    dot = functools.partial(jnp.dot, preferred_element_type=F32)
    return dot(high, t_high) + (dot(low, t_high) + dot(high, t_low))


def dot_pair(value, table):
    size = value.shape[0]
    both = jnp.dot(jnp.concatenate(split(value), axis=0), table[...], preferred_element_type=F32)
    return both[:size, :LANES] + (both[:size, LANES:] + both[size:, :LANES])


def kernel(
    lat_count, lon_count, cap_blocks,
    cut_hbm, tracer, zonal, north, ana_hbm, exp_hbm, syn_hbm, ends_hbm, out,
    cut_ref, q_in, zc, nc, ana, exp, syn, ends, q, tend,
    row_first, row_second, col_out, col_in, part, extra,
    load_sem, row_send, row_recv, col_send, col_recv, sum_send, sum_recv,
):
    rows, levels, cols = q_in.shape
    width = q.shape[2]
    total = cols * lon_count
    lat = lax.axis_index("lat")
    lon = lax.axis_index("lon")
    polar = jnp.logical_or(lat < cap_blocks, lat >= lat_count - cap_blocks)
    first = lat == 0
    last = lat == lat_count - 1
    east = lax.rem(lon + 1, lon_count)
    west = lax.rem(lon + lon_count - 1, lon_count)
    across = lax.rem(lon + lon_count // 2, lon_count)
    peers = [lax.rem(lon + step, lon_count) for step in range(lon_count)]
    steps = range(1, lon_count)
    order = [0, rows - 1, 1, rows - 2] + list(range(2, rows - 2))
    pieces = (((2, rows), (0, 2)), ((4, rows), (0, 4)))

    loads = []
    for index, (source, target) in enumerate(((tracer, q_in), (zonal, zc), (north, nc))):
        for row in range(rows):
            loads.append(pltpu.make_async_copy(
                source.at[:, row, :], target.at[row],
                load_sem.at[index * rows + row]))
    cut_in = pltpu.make_async_copy(cut_hbm, cut_ref, load_sem.at[3 * rows + 4])

    barrier = pltpu.get_barrier_semaphore()

    def greet(there):
        pl.semaphore_signal(barrier, inc=1, device_id=there, device_id_type=MESH)

    @pl.when(jnp.logical_not(first))
    def _():
        greet({"lat": lat - 1, "lon": lon})

    @pl.when(jnp.logical_not(last))
    def _():
        greet({"lat": lat + 1, "lon": lon})

    @pl.when(polar)
    def _():
        for step in steps:
            greet({"lat": lat, "lon": peers[step]})

    @pl.when(jnp.logical_not(polar))
    def _():
        greet({"lat": lat, "lon": east})
        greet({"lat": lat, "lon": west})

    tables_in = [
        pltpu.make_async_copy(ana_hbm, ana, load_sem.at[3 * rows]),
        pltpu.make_async_copy(exp_hbm, exp, load_sem.at[3 * rows + 1]),
        pltpu.make_async_copy(syn_hbm, syn, load_sem.at[3 * rows + 2]),
        pltpu.make_async_copy(ends_hbm, ends, load_sem.at[3 * rows + 3]),
    ]
    for load in loads[:2 * rows]:
        load.start()

    @pl.when(polar)
    def _():
        tables_in[0].start()

    for load in loads[2 * rows:]:
        load.start()

    edge = first.astype(jnp.int32) + last.astype(jnp.int32)
    sides = jnp.where(polar, lon_count - 1, 2)
    pl.semaphore_wait(barrier, 2 - edge + sides)

    def row_copy(turn, slot, row, there):
        source = tracer.at[:, row, :] if turn == 0 else q.at[row]
        target = row_first if turn == 0 else row_second
        return pltpu.make_async_remote_copy(
            source, target.at[slot],
            row_send.at[turn, 0 if row else 1], row_recv.at[turn, slot],
            device_id=there, device_id_type=MESH)

    def to_north(turn):
        return row_copy(turn, 0, rows - 1, {"lat": lat + 1, "lon": lon})

    def to_south(turn):
        return row_copy(turn, 1, 0, {"lat": lat - 1, "lon": lon})

    def over_north():
        return row_copy(0, 1, rows - 1, {"lat": lat, "lon": across})

    def over_south():
        return row_copy(0, 0, 0, {"lat": lat, "lon": across})

    @pl.when(last)
    def _():
        over_north().start()

    @pl.when(first)
    def _():
        over_south().start()

    @pl.when(jnp.logical_not(last))
    def _():
        to_north(0).start()

    @pl.when(jnp.logical_not(first))
    def _():
        to_south(0).start()

    @pl.when(polar)
    def _():
        for load in [cut_in] + tables_in[1:]:
            load.start()

    def rows_arrive(turn):
        @pl.when(jnp.logical_not(last))
        def _():
            to_south(turn).wait_recv()
            to_north(turn).wait_send()

        @pl.when(jnp.logical_not(first))
        def _():
            to_north(turn).wait_recv()
            to_south(turn).wait_send()

    def poles_arrive():
        @pl.when(last)
        def _():
            over_north().wait()

        @pl.when(first)
        def _():
            over_south().wait()

    lane = lax.broadcasted_iota(jnp.int32, (levels, LANES), 1)
    end_tile = (cols - 1) // LANES * LANES
    end_lane = (cols - 1) % LANES
    east_tile = cols // LANES * LANES
    west_tile = width - LANES

    def pack_cols(turn):
        packed = jnp.zeros((levels, LANES), F32)

        def put(packed, at, tile, came_from):
            return jnp.where(lane == at, pltpu.roll(tile, (at - came_from) % LANES, 1), packed)

        for row in range(rows):
            packed = put(packed, row, q[row, :, end_tile:end_tile + LANES], end_lane)
            packed = put(packed, rows + row, q[row, :, 0:LANES], 0)
        return packed

    def pack_factors(packed):
        for row in range(rows):
            tile = zc[row, :, end_tile:cols]
            if cols - end_tile < LANES:
                tile = jnp.concatenate(
                    [tile, jnp.zeros((levels, LANES - cols + end_tile), F32)], axis=1)
            factor = DIFFUSION - 0.5 * tile
            packed = jnp.where(
                lane == 2 * rows + row,
                pltpu.roll(factor, (2 * rows + row - end_lane) % LANES, 1), packed)
            factor = DIFFUSION + 0.5 * zc[row, :, 0:LANES]
            packed = jnp.where(
                lane == 3 * rows + row, pltpu.roll(factor, 3 * rows + row, 1), packed)
        return packed

    def place_cols(turn):
        from_west = col_in[turn, lon_count - 1]
        from_east = col_in[turn, 1]
        for row in range(rows):
            tile = q[row, :, east_tile:east_tile + LANES]
            moved = pltpu.roll(from_east, (cols % LANES - rows - row) % LANES, 1)
            q[row, :, east_tile:east_tile + LANES] = jnp.where(lane == cols % LANES, moved, tile)
            tile = q[row, :, west_tile:west_tile + LANES]
            moved = pltpu.roll(from_west, (LANES - 1 - row) % LANES, 1)
            q[row, :, west_tile:west_tile + LANES] = jnp.where(lane == LANES - 1, moved, tile)

    def col_copy(turn, step):
        return pltpu.make_async_remote_copy(
            col_out.at[turn], col_in.at[turn, lon_count - step],
            col_send.at[turn, step], col_recv.at[turn, lon_count - step],
            device_id={"lat": lat, "lon": peers[step]}, device_id_type=MESH)

    def col_arrival(turn, step):
        theirs = col_in.at[turn, step]
        return pltpu.make_async_remote_copy(
            theirs, theirs, col_send.at[turn, step], col_recv.at[turn, step],
            device_id={"lat": lat, "lon": peers[step]}, device_id_type=MESH)

    def sum_copy(turn, piece, step):
        low, high = pieces[turn][piece]
        return pltpu.make_async_remote_copy(
            part.at[turn, 0, low:high], part.at[turn, lon_count - step, low:high],
            sum_send.at[turn, piece, step], sum_recv.at[turn, piece, lon_count - step],
            device_id={"lat": lat, "lon": peers[step]}, device_id_type=MESH)

    def sum_arrival(turn, piece, step):
        low, high = pieces[turn][piece]
        theirs = part.at[turn, step, low:high]
        return pltpu.make_async_remote_copy(
            theirs, theirs, sum_send.at[turn, piece, step], sum_recv.at[turn, piece, step],
            device_id={"lat": lat, "lon": peers[step]}, device_id_type=MESH)

    def farthest_first(send):
        for distance in range(lon_count - 1, 0, -1):
            @pl.when(lon + distance < lon_count)
            def _():
                send(distance)

            @pl.when(lon - distance >= 0)
            def _():
                send(lon_count - distance)

    def stencil(turn, row):
        beyond = row_first if turn == 0 else row_second
        here = q[row]
        to_east = pltpu.roll(here, width - 1, 1)[:, :cols]
        to_west = pltpu.roll(here, 1, 1)[:, :cols]
        here = here[:, :cols]
        up = q[row + 1, :, :cols] if row < rows - 1 else beyond[1, :, :cols]
        down = q[row - 1, :, :cols] if row else beyond[0, :, :cols]
        return (-0.5 * zc[row] * (to_east - to_west)
                - 0.5 * nc[row] * (up - down)
                + DIFFUSION * (to_east + to_west + up + down - 4.0 * here))

    q[:, :, (width - LANES):] = jnp.zeros((rows, levels, LANES), F32)
    for load in loads[:rows]:
        load.wait()
    for row in range(rows):
        q[row, :, :cols] = q_in[row]

    @pl.when(jnp.logical_not(polar))
    def _():
        col_out[0] = pack_cols(0)
        for side in (1, lon_count - 1):
            col_copy(0, side).start()
        for load in loads[rows:]:
            load.wait()
        for side in (1, lon_count - 1):
            col_arrival(0, side).wait_recv()
        place_cols(0)
        rows_arrive(0)
        for row in range(rows):
            tend[row, :, :cols] = stencil(0, row)
        for row in range(rows):
            q[row, :, :cols] = q[row, :, :cols] + tend[row, :, :cols]
        to_north(1).start()
        to_south(1).start()
        col_out[1] = pack_cols(1)
        for side in (1, lon_count - 1):
            col_copy(1, side).start()
        for side in (1, lon_count - 1):
            col_arrival(1, side).wait_recv()
        rows_arrive(1)
        place_cols(1)
        for row in range(rows):
            out[:, row, :] = q[row, :, :cols] + stencil(1, row)
        for turn in range(2):
            for side in (1, lon_count - 1):
                col_copy(turn, side).wait_send()

    @pl.when(polar)
    def _():
        tend[:, :, (width - LANES):] = jnp.zeros((rows, levels, LANES), F32)
        for load in loads[rows:2 * rows]:
            load.wait()
        col_out[0] = pack_factors(pack_cols(0))
        farthest_first(lambda step: col_copy(0, step).start())
        for load in loads[2 * rows:] + tables_in[:1]:
            load.wait()

        def analyse(turn, piece):
            low, high = pieces[turn][piece]
            count = high - low
            for slot in range(low, high):
                tend[slot, :, :cols] = stencil(turn, order[slot])
            found = dot_pair(tend[low:high].reshape(count * levels, width), ana)
            part[turn, 0, low:high] = found.reshape(count, levels, LANES)
            farthest_first(lambda step: sum_copy(turn, piece, step).start())

        def collect(turn, piece):
            low, high = pieces[turn][piece]
            for step in steps:
                sum_arrival(turn, piece, step).wait_recv()
            count = high - low
            gathered = jnp.concatenate(
                [part[turn, step, low:high].reshape(count * levels, LANES)
                 for step in range(lon_count)], axis=1)
            summed = dot3(gathered, exp).reshape(count, levels, 2 * KMAX)
            result = []
            for slot in range(low, high):
                total_sum = summed[slot - low]
                if turn == 0:
                    total_sum = total_sum + extra[slot]
                result.append(total_sum * keep[order[slot]])
            return result

        def synthesise(parts):
            return dot3(jnp.concatenate(parts, axis=0), syn).reshape(len(parts), levels, width)

        analyse(0, 0)
        rows_arrive(0)
        poles_arrive()
        analyse(0, 1)

        for load in tables_in[1:] + [cut_in]:
            load.wait()
        offset = jnp.where(
            lat < cap_blocks, lat * rows, (lat - lat_count + 2 * cap_blocks) * rows)
        mode = lax.broadcasted_iota(jnp.int32, (1, 2 * KMAX), 1) % KMAX
        weight = jnp.where(mode == 0, 1.0 / total, 2.0 / total).astype(F32)
        keep = [jnp.where(mode < cut_ref[offset + row], weight, 0.0) for row in range(rows)]
        parity = 1.0 - 2.0 * (lax.broadcasted_iota(jnp.int32, (1, 2 * KMAX), 1) % 2).astype(F32)

        for step in steps:
            col_arrival(0, step).wait_recv()
        col_in[0, 0] = col_out[0]
        place_cols(0)
        packed = [col_in[0, step] for step in range(lon_count)]
        added = [jnp.zeros((levels, 2 * KMAX), F32) for _ in range(rows)]
        for step in range(lon_count):
            behind = packed[step - 1]
            ahead = packed[(step + 1) % lon_count]
            at_last = packed[step] * pltpu.roll(ahead, rows, 1)
            at_first = packed[step] * pltpu.roll(behind, 3 * rows, 1)
            for row in range(rows):
                column = at_last[:, 2 * rows + row:2 * rows + row + 1]
                added[row] = added[row] + column * ends[step, 1:2, :]
                column = at_first[:, 3 * rows + row:3 * rows + row + 1]
                added[row] = added[row] + column * ends[step, 0:1, :]
        for slot in range(rows):
            extra[slot] = added[order[slot]]

        low, high = pieces[0][0]
        filtered = synthesise(collect(0, 0))
        for slot in range(low, high):
            q[order[slot]] = q[order[slot]] + filtered[slot - low]
        analyse(1, 0)

        local = collect(0, 1)
        pole_row = jnp.where(first, local[0], local[1]) * parity
        filtered = synthesise(local + [pole_row])
        q[0] = q[0] + filtered[0]
        q[rows - 1] = q[rows - 1] + filtered[1]

        @pl.when(jnp.logical_not(last))
        def _():
            to_north(1).start()

        @pl.when(jnp.logical_not(first))
        def _():
            to_south(1).start()

        @pl.when(last)
        def _():
            row_second[1, :, :cols] = row_first[1] + filtered[2, :, :cols]

        @pl.when(first)
        def _():
            row_second[0, :, :cols] = row_first[0] + filtered[2, :, :cols]

        rows_arrive(1)
        analyse(1, 1)
        for piece in range(2):
            low, high = pieces[1][piece]
            filtered = synthesise(collect(1, piece))
            for slot in range(low, high):
                row = order[slot]
                out[:, row, :] = q[row, :, :cols] + filtered[slot - low, :, :cols]
        for step in steps:
            col_copy(0, step).wait_send()
            for turn in range(2):
                for piece in range(2):
                    sum_copy(turn, piece, step).wait_send()


def shards(tracer, zonal_courant, north_courant, cutoff):
    levels, rows, cols = tracer.shape
    lat_count = lax.axis_size("lat")
    lon_count = lax.axis_size("lon")
    cap_blocks = lat_count // 8
    width = -(-(cols + 2) // LANES) * LANES
    analysis, expand, synthesis, ends = tables(cols, width, lon_count)
    dma = pltpu.SemaphoreType.DMA
    anywhere = pl.BlockSpec(memory_space=pl.ANY)
    return pl.pallas_call(
        functools.partial(kernel, lat_count, lon_count, cap_blocks),
        out_shape=pltpu.VMEM(tracer.shape, F32),
        in_specs=[anywhere] * 8,
        out_specs=pl.BlockSpec(memory_space=pltpu.VMEM),
        scratch_shapes=[
            pltpu.SMEM(cutoff.shape, jnp.int32),
            pltpu.VMEM((rows, levels, cols), F32),
            pltpu.VMEM((rows, levels, cols), F32),
            pltpu.VMEM((rows, levels, cols), F32),
            pltpu.VMEM(analysis.shape, BF16),
            pltpu.VMEM(expand.shape, BF16),
            pltpu.VMEM(synthesis.shape, BF16),
            pltpu.VMEM(ends.shape, F32),
            pltpu.VMEM((rows, levels, width), F32),
            pltpu.VMEM((rows, levels, width), F32),
            pltpu.VMEM((2, levels, cols), F32),
            pltpu.VMEM((2, levels, width), F32),
            pltpu.VMEM((2, levels, LANES), F32),
            pltpu.VMEM((2, lon_count, levels, LANES), F32),
            pltpu.VMEM((2, lon_count, rows, levels, LANES), F32),
            pltpu.VMEM((rows, levels, 2 * KMAX), F32),
            dma((3 * rows + 5,)),
            dma((2, 2)), dma((2, 2)), dma((2, lon_count)), dma((2, lon_count)),
            dma((2, 2, lon_count)), dma((2, 2, lon_count)),
        ],
        compiler_params=pltpu.CompilerParams(collective_id=0, has_side_effects=True),
    )(cutoff, tracer, zonal_courant, north_courant,
      jnp.asarray(analysis), jnp.asarray(expand), jnp.asarray(synthesis), jnp.asarray(ends))


def solution(mesh):
    return jax.shard_map(
        shards,
        mesh=mesh,
        in_specs=(P(None, "lat", "lon"), P(None, "lat", "lon"), P(None, "lat", "lon"), P()),
        out_specs=P(None, "lat", "lon"),
        check_vma=False,
    )
```

```python
import functools
import math

import jax
import jax.numpy as jnp
import numpy as np
from jax import lax
from jax.experimental import pallas as pl
from jax.experimental.pallas import tpu as pltpu
from jax.sharding import PartitionSpec as P

KMAX = 128
DIFFUSION = 0.2
LANES = 128
MESH = pl.DeviceIdType.MESH
F32 = jnp.float32
BF16 = jnp.bfloat16


def split_table(table):
    high = table.astype(np.float32).astype(BF16)
    low = (table - high.astype(np.float64)).astype(np.float32).astype(BF16)
    return np.stack([high, low])


def trig(columns, total):
    modes = np.arange(KMAX)
    angle = (columns[:, None] * modes[None, :] % total) * (2.0 * math.pi / total)
    return np.concatenate([np.cos(angle), np.sin(angle)], axis=1)


def window_basis(cols, total):
    bandwidth = (KMAX - 0.5) / total
    place = np.arange(cols)
    operator = np.diag(((cols - 1 - 2 * place) / 2.0) ** 2 * math.cos(2.0 * math.pi * bandwidth))
    beside = np.arange(1, cols) * (cols - np.arange(1, cols)) / 2.0
    operator = operator + np.diag(beside, 1) + np.diag(beside, -1)
    vectors = np.linalg.eigh(operator)[1][:, ::-1]
    half = vectors[:(cols + 1) // 2]
    peak = np.take_along_axis(half, np.abs(half).argmax(0)[None], 0)[0]
    return vectors * np.where(peak < 0, -1.0, 1.0)


def tables(cols, width, lon_count):
    total = cols * lon_count
    kept = min(LANES, cols)
    basis = np.zeros((width, LANES))
    basis[:cols, :kept] = window_basis(cols, total)[:, :kept]
    analysis = np.concatenate(list(split_table(basis)), axis=1)
    expand = np.zeros((lon_count, LANES, 2 * KMAX))
    for step in range(lon_count):
        expand[step] = basis[:cols].T @ trig(np.arange(cols) + step * cols, total)
    expand = split_table(expand.reshape(lon_count * LANES, 2 * KMAX))
    lane = np.arange(width)
    lane = np.where(lane == width - 1, -1, lane)
    synthesis = split_table(trig(lane, total).T.copy())
    ends = np.zeros((lon_count, 8, 2 * KMAX), np.float32)
    ends[:, 0] = trig(np.arange(lon_count) * cols, total)
    ends[:, 1] = trig(np.arange(lon_count) * cols + cols - 1, total)
    return analysis, expand, synthesis, ends


def split(value):
    high = value.astype(BF16)
    low = (value - high.astype(F32)).astype(BF16)
    return high, low


def dot3(value, table):
    high, low = split(value)
    t_high = table[0]
    t_low = table[1]
    dot = functools.partial(jnp.dot, preferred_element_type=F32)
    return dot(high, t_high) + (dot(low, t_high) + dot(high, t_low))


def dot_pair(value, table):
    size = value.shape[0]
    both = jnp.dot(jnp.concatenate(split(value), axis=0), table[...], preferred_element_type=F32)
    return both[:size, :LANES] + (both[:size, LANES:] + both[size:, :LANES])


def kernel(
    lat_count, lon_count, cap_blocks,
    cut_hbm, tracer, zonal, north, ana_hbm, exp_hbm, syn_hbm, ends_hbm, out,
    cut_ref, q_in, zc, nc, ana, exp, syn, ends, q, tend,
    row_first, row_second, col_out, col_in, part, extra,
    load_sem, ready, row_send, row_recv, col_send, col_recv, sum_send, sum_recv,
):
    rows, levels, cols = q_in.shape
    width = q.shape[2]
    total = cols * lon_count
    lat = lax.axis_index("lat")
    lon = lax.axis_index("lon")
    polar = jnp.logical_or(lat < cap_blocks, lat >= lat_count - cap_blocks)
    first = lat == 0
    last = lat == lat_count - 1
    southern = 2 * lat < lat_count
    border_south = lat == cap_blocks
    border_north = lat == lat_count - 1 - cap_blocks
    beyond_south = lat == cap_blocks + 1
    beyond_north = lat == lat_count - 2 - cap_blocks
    east = lax.rem(lon + 1, lon_count)
    west = lax.rem(lon + lon_count - 1, lon_count)
    across = lax.rem(lon + lon_count // 2, lon_count)
    peers = [lax.rem(lon + step, lon_count) for step in range(lon_count)]
    steps = range(1, lon_count)
    order = [0, rows - 1, 1, rows - 2] + list(range(2, rows - 2))
    pieces = (((2, rows), (0, 2)), ((4, rows), (0, 4)))

    loads = []
    for index, (source, target) in enumerate(((tracer, q_in), (zonal, zc), (north, nc))):
        for row in range(rows):
            loads.append(pltpu.make_async_copy(
                source.at[:, row, :], target.at[row],
                load_sem.at[index * rows + row]))
    cut_in = pltpu.make_async_copy(cut_hbm, cut_ref, load_sem.at[3 * rows + 4])

    barrier = pltpu.get_barrier_semaphore()

    def greet(there):
        pl.semaphore_signal(barrier, inc=1, device_id=there, device_id_type=MESH)

    @pl.when(jnp.logical_not(jnp.logical_or(first, beyond_south)))
    def _():
        greet({"lat": lat - 1, "lon": lon})

    @pl.when(jnp.logical_not(jnp.logical_or(last, beyond_north)))
    def _():
        greet({"lat": lat + 1, "lon": lon})

    @pl.when(polar)
    def _():
        for step in steps:
            greet({"lat": lat, "lon": peers[step]})

    @pl.when(jnp.logical_not(polar))
    def _():
        greet({"lat": lat, "lon": east})
        greet({"lat": lat, "lon": west})

    tables_in = [
        pltpu.make_async_copy(ana_hbm, ana, load_sem.at[3 * rows]),
        pltpu.make_async_copy(exp_hbm, exp, load_sem.at[3 * rows + 1]),
        pltpu.make_async_copy(syn_hbm, syn, load_sem.at[3 * rows + 2]),
        pltpu.make_async_copy(ends_hbm, ends, load_sem.at[3 * rows + 3]),
    ]
    for load in loads[:2 * rows]:
        load.start()

    @pl.when(polar)
    def _():
        tables_in[0].start()

    for load in loads[2 * rows:]:
        load.start()

    edge = jnp.logical_or(
        jnp.logical_or(first, last), jnp.logical_or(border_south, border_north)).astype(jnp.int32)
    sides = jnp.where(polar, lon_count - 1, 2)
    pl.semaphore_wait(barrier, 2 - edge + sides)

    def row_copy(turn, slot, row, there):
        source = tracer.at[:, row, :] if turn == 0 else q.at[row]
        target = row_first if turn == 0 else row_second
        return pltpu.make_async_remote_copy(
            source, target.at[slot],
            row_send.at[turn, 0 if row else 1], row_recv.at[turn, slot],
            device_id=there, device_id_type=MESH)

    def to_north(turn):
        return row_copy(turn, 0, rows - 1, {"lat": lat + 1, "lon": lon})

    def to_south(turn):
        return row_copy(turn, 1, 0, {"lat": lat - 1, "lon": lon})

    def over_north():
        return row_copy(0, 1, rows - 1, {"lat": lat, "lon": across})

    def over_south():
        return row_copy(0, 0, 0, {"lat": lat, "lon": across})

    @pl.when(last)
    def _():
        over_north().start()

    @pl.when(first)
    def _():
        over_south().start()

    @pl.when(jnp.logical_not(jnp.logical_or(last, border_south)))
    def _():
        to_north(0).start()

    @pl.when(jnp.logical_not(jnp.logical_or(first, border_north)))
    def _():
        to_south(0).start()

    def report(there):
        pl.semaphore_signal(
            ready, inc=1, device_id={"lat": there, "lon": lon}, device_id_type=MESH)

    @pl.when(beyond_south)
    def _():
        report(lat - 1)

    @pl.when(beyond_north)
    def _():
        report(lat + 1)

    @pl.when(polar)
    def _():
        for load in [cut_in] + tables_in[1:]:
            load.start()

    def rows_arrive(turn):
        @pl.when(jnp.logical_not(last))
        def _():
            to_south(turn).wait_recv()

        @pl.when(jnp.logical_not(first))
        def _():
            to_north(turn).wait_recv()

    def rows_left(turn):
        @pl.when(jnp.logical_not(last))
        def _():
            to_north(turn).wait_send()

        @pl.when(jnp.logical_not(first))
        def _():
            to_south(turn).wait_send()

    def poles_left():
        @pl.when(last)
        def _():
            over_north().wait_send()

        @pl.when(first)
        def _():
            over_south().wait_send()

    def poles_arrive():
        @pl.when(last)
        def _():
            over_north().wait_recv()

        @pl.when(first)
        def _():
            over_south().wait_recv()

    lane = lax.broadcasted_iota(jnp.int32, (levels, LANES), 1)
    end_tile = (cols - 1) // LANES * LANES
    end_lane = (cols - 1) % LANES
    east_tile = cols // LANES * LANES
    west_tile = width - LANES

    def pack_cols(turn):
        packed = jnp.zeros((levels, LANES), F32)

        def put(packed, at, tile, came_from):
            return jnp.where(lane == at, pltpu.roll(tile, (at - came_from) % LANES, 1), packed)

        for row in range(rows):
            packed = put(packed, row, q[row, :, end_tile:end_tile + LANES], end_lane)
            packed = put(packed, rows + row, q[row, :, 0:LANES], 0)
        return packed

    def pack_factors(packed):
        for row in range(rows):
            tile = zc[row, :, end_tile:cols]
            if cols - end_tile < LANES:
                tile = jnp.concatenate(
                    [tile, jnp.zeros((levels, LANES - cols + end_tile), F32)], axis=1)
            factor = DIFFUSION - 0.5 * tile
            packed = jnp.where(
                lane == 2 * rows + row,
                pltpu.roll(factor, (2 * rows + row - end_lane) % LANES, 1), packed)
            factor = DIFFUSION + 0.5 * zc[row, :, 0:LANES]
            packed = jnp.where(
                lane == 3 * rows + row, pltpu.roll(factor, 3 * rows + row, 1), packed)
        return packed

    def place_cols(turn):
        from_west = col_in[turn, lon_count - 1]
        from_east = col_in[turn, 1]
        for row in range(rows):
            tile = q[row, :, east_tile:east_tile + LANES]
            moved = pltpu.roll(from_east, (cols % LANES - rows - row) % LANES, 1)
            q[row, :, east_tile:east_tile + LANES] = jnp.where(lane == cols % LANES, moved, tile)
            tile = q[row, :, west_tile:west_tile + LANES]
            moved = pltpu.roll(from_west, (LANES - 1 - row) % LANES, 1)
            q[row, :, west_tile:west_tile + LANES] = jnp.where(lane == LANES - 1, moved, tile)

    def col_copy(turn, step):
        return pltpu.make_async_remote_copy(
            col_out.at[turn], col_in.at[turn, lon_count - step],
            col_send.at[turn, step], col_recv.at[turn, lon_count - step],
            device_id={"lat": lat, "lon": peers[step]}, device_id_type=MESH)

    def col_arrival(turn, step):
        theirs = col_in.at[turn, step]
        return pltpu.make_async_remote_copy(
            theirs, theirs, col_send.at[turn, step], col_recv.at[turn, step],
            device_id={"lat": lat, "lon": peers[step]}, device_id_type=MESH)

    def sum_copy(turn, piece, step):
        low, high = pieces[turn][piece]
        return pltpu.make_async_remote_copy(
            part.at[turn, 0, low:high], part.at[turn, lon_count - step, low:high],
            sum_send.at[turn, piece, step], sum_recv.at[turn, piece, lon_count - step],
            device_id={"lat": lat, "lon": peers[step]}, device_id_type=MESH)

    def sum_arrival(turn, piece, step):
        low, high = pieces[turn][piece]
        theirs = part.at[turn, step, low:high]
        return pltpu.make_async_remote_copy(
            theirs, theirs, sum_send.at[turn, piece, step], sum_recv.at[turn, piece, step],
            device_id={"lat": lat, "lon": peers[step]}, device_id_type=MESH)

    def farthest_first(send):
        for distance in range(lon_count - 1, 0, -1):
            @pl.when(lon + distance < lon_count)
            def _():
                send(distance)

            @pl.when(lon - distance >= 0)
            def _():
                send(lon_count - distance)

    def stencil(turn, row):
        beyond = row_first if turn == 0 else row_second
        here = q[row]
        to_east = pltpu.roll(here, width - 1, 1)[:, :cols]
        to_west = pltpu.roll(here, 1, 1)[:, :cols]
        here = here[:, :cols]
        up = q[row + 1, :, :cols] if row < rows - 1 else beyond[1, :, :cols]
        down = q[row - 1, :, :cols] if row else beyond[0, :, :cols]
        return (-0.5 * zc[row] * (to_east - to_west)
                - 0.5 * nc[row] * (up - down)
                + DIFFUSION * (to_east + to_west + up + down - 4.0 * here))

    q[:, :, (width - LANES):] = jnp.zeros((rows, levels, LANES), F32)
    for load in loads[:rows]:
        load.wait()
    for row in range(rows):
        q[row, :, :cols] = q_in[row]

    @pl.when(jnp.logical_not(polar))
    def _():
        col_out[0] = pack_cols(0)
        for side in (1, lon_count - 1):
            col_copy(0, side).start()
        for load in loads[rows:]:
            load.wait()
        for side in (1, lon_count - 1):
            col_arrival(0, side).wait_recv()
        place_cols(0)
        for row in range(1, rows - 1):
            tend[row, :, :cols] = stencil(0, row)

        def advance_edge(row):
            if row:
                to_south(0).wait_recv()
            else:
                to_north(0).wait_recv()
            q[row, :, :cols] = q[row, :, :cols] + stencil(0, row)
            if row:
                to_north(1).start()
            else:
                to_south(1).start()

        @pl.when(southern)
        def _():
            advance_edge(0)

            @pl.when(border_south)
            def _():
                pl.semaphore_wait(ready, 1)
                to_north(0).start()

            advance_edge(rows - 1)

        @pl.when(jnp.logical_not(southern))
        def _():
            advance_edge(rows - 1)

            @pl.when(border_north)
            def _():
                pl.semaphore_wait(ready, 1)
                to_south(0).start()

            advance_edge(0)

        for row in range(1, rows - 1):
            q[row, :, :cols] = q[row, :, :cols] + tend[row, :, :cols]
        col_out[1] = pack_cols(1)
        for side in (1, lon_count - 1):
            col_copy(1, side).start()
        for side in (1, lon_count - 1):
            col_arrival(1, side).wait_recv()
        rows_left(1)
        place_cols(1)
        for row in range(1, rows - 1):
            out[:, row, :] = q[row, :, :cols] + stencil(1, row)
        rows_arrive(1)
        for row in (0, rows - 1):
            out[:, row, :] = q[row, :, :cols] + stencil(1, row)
        rows_left(0)
        for turn in range(2):
            for side in (1, lon_count - 1):
                col_copy(turn, side).wait_send()

    @pl.when(polar)
    def _():
        tend[:, :, (width - LANES):] = jnp.zeros((rows, levels, LANES), F32)
        for load in loads[rows:2 * rows]:
            load.wait()
        col_out[0] = pack_factors(pack_cols(0))
        farthest_first(lambda step: col_copy(0, step).start())
        for load in loads[2 * rows:] + tables_in[:1]:
            load.wait()

        def analyse(turn, piece):
            low, high = pieces[turn][piece]
            count = high - low
            for slot in range(low, high):
                tend[slot, :, :cols] = stencil(turn, order[slot])
            found = dot_pair(tend[low:high].reshape(count * levels, width), ana)
            part[turn, 0, low:high] = found.reshape(count, levels, LANES)
            farthest_first(lambda step: sum_copy(turn, piece, step).start())

        def collect(turn, piece):
            low, high = pieces[turn][piece]
            for step in steps:
                sum_arrival(turn, piece, step).wait_recv()
            count = high - low
            gathered = jnp.concatenate(
                [part[turn, step, low:high].reshape(count * levels, LANES)
                 for step in range(lon_count)], axis=1)
            summed = dot3(gathered, exp).reshape(count, levels, 2 * KMAX)
            result = []
            for slot in range(low, high):
                total_sum = summed[slot - low]
                if turn == 0:
                    total_sum = total_sum + extra[slot]
                result.append(total_sum * keep[order[slot]])
            return result

        def synthesise(parts):
            return dot3(jnp.concatenate(parts, axis=0), syn).reshape(len(parts), levels, width)

        analyse(0, 0)
        rows_arrive(0)
        poles_arrive()
        analyse(0, 1)

        for load in tables_in[1:] + [cut_in]:
            load.wait()
        offset = jnp.where(
            lat < cap_blocks, lat * rows, (lat - lat_count + 2 * cap_blocks) * rows)
        mode = lax.broadcasted_iota(jnp.int32, (1, 2 * KMAX), 1) % KMAX
        weight = jnp.where(mode == 0, 1.0 / total, 2.0 / total).astype(F32)
        keep = [jnp.where(mode < cut_ref[offset + row], weight, 0.0) for row in range(rows)]
        parity = 1.0 - 2.0 * (lax.broadcasted_iota(jnp.int32, (1, 2 * KMAX), 1) % 2).astype(F32)

        for step in steps:
            col_arrival(0, step).wait_recv()
        col_in[0, 0] = col_out[0]
        place_cols(0)
        packed = [col_in[0, step] for step in range(lon_count)]
        added = [jnp.zeros((levels, 2 * KMAX), F32) for _ in range(rows)]
        for step in range(lon_count):
            behind = packed[step - 1]
            ahead = packed[(step + 1) % lon_count]
            at_last = packed[step] * pltpu.roll(ahead, rows, 1)
            at_first = packed[step] * pltpu.roll(behind, 3 * rows, 1)
            for row in range(rows):
                column = at_last[:, 2 * rows + row:2 * rows + row + 1]
                added[row] = added[row] + column * ends[step, 1:2, :]
                column = at_first[:, 3 * rows + row:3 * rows + row + 1]
                added[row] = added[row] + column * ends[step, 0:1, :]
        for slot in range(rows):
            extra[slot] = added[order[slot]]

        low, high = pieces[0][0]
        filtered = synthesise(collect(0, 0))
        for slot in range(low, high):
            q[order[slot]] = q[order[slot]] + filtered[slot - low]
        analyse(1, 0)

        local = collect(0, 1)
        pole_row = jnp.where(first, local[0], local[1]) * parity
        filtered = synthesise(local + [pole_row])
        q[0] = q[0] + filtered[0]
        q[rows - 1] = q[rows - 1] + filtered[1]

        @pl.when(jnp.logical_not(last))
        def _():
            to_north(1).start()

        @pl.when(jnp.logical_not(first))
        def _():
            to_south(1).start()

        @pl.when(last)
        def _():
            row_second[1, :, :cols] = row_first[1] + filtered[2, :, :cols]

        @pl.when(first)
        def _():
            row_second[0, :, :cols] = row_first[0] + filtered[2, :, :cols]

        rows_arrive(1)
        analyse(1, 1)
        for piece in range(2):
            low, high = pieces[1][piece]
            filtered = synthesise(collect(1, piece))
            for slot in range(low, high):
                row = order[slot]
                out[:, row, :] = q[row, :, :cols] + filtered[slot - low, :, :cols]
        rows_left(0)
        rows_left(1)
        poles_left()
        for step in steps:
            col_copy(0, step).wait_send()
            for turn in range(2):
                for piece in range(2):
                    sum_copy(turn, piece, step).wait_send()


def shards(tracer, zonal_courant, north_courant, cutoff):
    levels, rows, cols = tracer.shape
    lat_count = lax.axis_size("lat")
    lon_count = lax.axis_size("lon")
    cap_blocks = lat_count // 8
    width = -(-(cols + 2) // LANES) * LANES
    analysis, expand, synthesis, ends = tables(cols, width, lon_count)
    dma = pltpu.SemaphoreType.DMA
    anywhere = pl.BlockSpec(memory_space=pl.ANY)
    return pl.pallas_call(
        functools.partial(kernel, lat_count, lon_count, cap_blocks),
        out_shape=pltpu.VMEM(tracer.shape, F32),
        in_specs=[anywhere] * 8,
        out_specs=pl.BlockSpec(memory_space=pltpu.VMEM),
        scratch_shapes=[
            pltpu.SMEM(cutoff.shape, jnp.int32),
            pltpu.VMEM((rows, levels, cols), F32),
            pltpu.VMEM((rows, levels, cols), F32),
            pltpu.VMEM((rows, levels, cols), F32),
            pltpu.VMEM(analysis.shape, BF16),
            pltpu.VMEM(expand.shape, BF16),
            pltpu.VMEM(synthesis.shape, BF16),
            pltpu.VMEM(ends.shape, F32),
            pltpu.VMEM((rows, levels, width), F32),
            pltpu.VMEM((rows, levels, width), F32),
            pltpu.VMEM((2, levels, cols), F32),
            pltpu.VMEM((2, levels, width), F32),
            pltpu.VMEM((2, levels, LANES), F32),
            pltpu.VMEM((2, lon_count, levels, LANES), F32),
            pltpu.VMEM((2, lon_count, rows, levels, LANES), F32),
            pltpu.VMEM((rows, levels, 2 * KMAX), F32),
            dma((3 * rows + 5,)), pltpu.SemaphoreType.REGULAR,
            dma((2, 2)), dma((2, 2)), dma((2, lon_count)), dma((2, lon_count)),
            dma((2, 2, lon_count)), dma((2, 2, lon_count)),
        ],
        compiler_params=pltpu.CompilerParams(collective_id=0, has_side_effects=True),
    )(cutoff, tracer, zonal_courant, north_courant,
      jnp.asarray(analysis), jnp.asarray(expand), jnp.asarray(synthesis), jnp.asarray(ends))


def solution(mesh):
    return jax.shard_map(
        shards,
        mesh=mesh,
        in_specs=(P(None, "lat", "lon"), P(None, "lat", "lon"), P(None, "lat", "lon"), P()),
        out_specs=P(None, "lat", "lon"),
        check_vma=False,
    )
```

```python
import functools
import math

import jax
import jax.numpy as jnp
import numpy as np
from jax import lax
from jax.experimental import pallas as pl
from jax.experimental.pallas import tpu as pltpu
from jax.sharding import PartitionSpec as P

KMAX = 128
DIFFUSION = 0.2
LANES = 128
QUARTER = LANES // 4
KEPT = 3 * QUARTER
MESH = pl.DeviceIdType.MESH
F32 = jnp.float32
BF16 = jnp.bfloat16


def split_table(table):
    high = table.astype(np.float32).astype(BF16)
    low = (table - high.astype(np.float64)).astype(np.float32).astype(BF16)
    return np.stack([high, low])


def trig(columns, total):
    modes = np.arange(KMAX)
    angle = (columns[:, None] * modes[None, :] % total) * (2.0 * math.pi / total)
    return np.concatenate([np.cos(angle), np.sin(angle)], axis=1)


def window_basis(cols, total):
    bandwidth = (KMAX - 0.5) / total
    place = np.arange(cols)
    operator = np.diag(((cols - 1 - 2 * place) / 2.0) ** 2 * math.cos(2.0 * math.pi * bandwidth))
    beside = np.arange(1, cols) * (cols - np.arange(1, cols)) / 2.0
    operator = operator + np.diag(beside, 1) + np.diag(beside, -1)
    vectors = np.linalg.eigh(operator)[1][:, ::-1]
    half = vectors[:(cols + 1) // 2]
    peak = np.take_along_axis(half, np.abs(half).argmax(0)[None], 0)[0]
    return vectors * np.where(peak < 0, -1.0, 1.0)


def tables(cols, width, lon_count):
    total = cols * lon_count
    basis = np.zeros((width, LANES))
    basis[:cols, :KEPT] = window_basis(cols, total)[:, :KEPT]
    waves = trig(np.arange(cols), total)
    assert np.abs(waves - basis[:cols] @ (basis[:cols].T @ waves)).max() < 1e-11
    analysis = np.concatenate(list(split_table(basis)), axis=1)
    expand = np.zeros((lon_count, LANES, 2 * KMAX))
    for step in range(lon_count):
        expand[step] = basis[:cols].T @ trig(np.arange(cols) + step * cols, total)
    expand = split_table(expand.reshape(lon_count * LANES, 2 * KMAX))
    lane = np.arange(width)
    lane = np.where(lane == width - 1, -1, lane)
    synthesis = split_table(trig(lane, total).T.copy())
    ends = np.zeros((lon_count, 8, 2 * KMAX), np.float32)
    ends[:, 0] = trig(np.arange(lon_count) * cols, total)
    ends[:, 1] = trig(np.arange(lon_count) * cols + cols - 1, total)
    return analysis, expand, synthesis, ends


def split(value):
    high = value.astype(BF16)
    low = (value - high.astype(F32)).astype(BF16)
    return high, low


def dot3(value, table):
    high, low = split(value)
    t_high = table[0]
    t_low = table[1]
    dot = functools.partial(jnp.dot, preferred_element_type=F32)
    return dot(high, t_high) + (dot(low, t_high) + dot(high, t_low))


def dot_pair(value, table):
    size = value.shape[0]
    both = jnp.dot(jnp.concatenate(split(value), axis=0), table[...], preferred_element_type=F32)
    return both[:size, :LANES] + (both[:size, LANES:] + both[size:, :LANES])


def packed_tiles(count):
    return count // 4 * 3 + count % 4


def pack(values, lane):
    tiles = []
    while len(values) >= 4:
        fourth = values[3]
        for place in range(3):
            moved = pltpu.roll(fourth, KEPT - place * QUARTER, 1)
            tiles.append(jnp.where(lane >= KEPT, moved, values[place]))
        values = values[4:]
    return tiles + values


def unpack(tiles, count, lane):
    values = []
    while count >= 4:
        moved = [pltpu.roll(tiles[place], (place + 1) * QUARTER, 1) for place in range(3)]
        fourth = jnp.where(
            lane < QUARTER, moved[0], jnp.where(lane < 2 * QUARTER, moved[1], moved[2]))
        values += tiles[:3] + [fourth]
        tiles = tiles[3:]
        count -= 4
    return values + tiles


def kernel(
    lat_count, lon_count, cap_blocks,
    cut_hbm, tracer, zonal, north, ana_hbm, exp_hbm, syn_hbm, ends_hbm, out,
    cut_ref, q_in, zc, nc, ana, exp, syn, ends, q, tend,
    row_first, row_second, col_out, col_in, part, extra,
    load_sem, ready, row_send, row_recv, col_send, col_recv, sum_send, sum_recv,
):
    rows, levels, cols = q_in.shape
    width = q.shape[2]
    total = cols * lon_count
    lat = lax.axis_index("lat")
    lon = lax.axis_index("lon")
    polar = jnp.logical_or(lat < cap_blocks, lat >= lat_count - cap_blocks)
    first = lat == 0
    last = lat == lat_count - 1
    southern = 2 * lat < lat_count
    border_south = lat == cap_blocks
    border_north = lat == lat_count - 1 - cap_blocks
    beyond_south = lat == cap_blocks + 1
    beyond_north = lat == lat_count - 2 - cap_blocks
    east = lax.rem(lon + 1, lon_count)
    west = lax.rem(lon + lon_count - 1, lon_count)
    across = lax.rem(lon + lon_count // 2, lon_count)
    peers = [lax.rem(lon + step, lon_count) for step in range(lon_count)]
    steps = range(1, lon_count)
    order = [0, rows - 1, 1, rows - 2] + list(range(2, rows - 2))
    pieces = (((2, rows), (0, 2)), ((4, rows), (0, 4)))
    spans = [[], []]
    for turn in range(2):
        used = 0
        for low, high in pieces[turn]:
            spans[turn].append((used, used + packed_tiles(high - low)))
            used = spans[turn][-1][1]

    loads = []
    for index, (source, target) in enumerate(((tracer, q_in), (zonal, zc), (north, nc))):
        for row in range(rows):
            loads.append(pltpu.make_async_copy(
                source.at[:, row, :], target.at[row],
                load_sem.at[index * rows + row]))
    cut_in = pltpu.make_async_copy(cut_hbm, cut_ref, load_sem.at[3 * rows + 4])

    barrier = pltpu.get_barrier_semaphore()

    def greet(there):
        pl.semaphore_signal(barrier, inc=1, device_id=there, device_id_type=MESH)

    @pl.when(jnp.logical_not(jnp.logical_or(first, beyond_south)))
    def _():
        greet({"lat": lat - 1, "lon": lon})

    @pl.when(jnp.logical_not(jnp.logical_or(last, beyond_north)))
    def _():
        greet({"lat": lat + 1, "lon": lon})

    @pl.when(polar)
    def _():
        for step in steps:
            greet({"lat": lat, "lon": peers[step]})

    @pl.when(jnp.logical_not(polar))
    def _():
        greet({"lat": lat, "lon": east})
        greet({"lat": lat, "lon": west})

    tables_in = [
        pltpu.make_async_copy(ana_hbm, ana, load_sem.at[3 * rows]),
        pltpu.make_async_copy(exp_hbm, exp, load_sem.at[3 * rows + 1]),
        pltpu.make_async_copy(syn_hbm, syn, load_sem.at[3 * rows + 2]),
        pltpu.make_async_copy(ends_hbm, ends, load_sem.at[3 * rows + 3]),
    ]
    for load in loads[:2 * rows]:
        load.start()

    @pl.when(polar)
    def _():
        tables_in[0].start()

    for load in loads[2 * rows:]:
        load.start()

    edge = jnp.logical_or(
        jnp.logical_or(first, last), jnp.logical_or(border_south, border_north)).astype(jnp.int32)
    sides = jnp.where(polar, lon_count - 1, 2)
    pl.semaphore_wait(barrier, 2 - edge + sides)

    def row_copy(turn, slot, row, there):
        source = tracer.at[:, row, :] if turn == 0 else q.at[row]
        target = row_first if turn == 0 else row_second
        return pltpu.make_async_remote_copy(
            source, target.at[slot],
            row_send.at[turn, 0 if row else 1], row_recv.at[turn, slot],
            device_id=there, device_id_type=MESH)

    def to_north(turn):
        return row_copy(turn, 0, rows - 1, {"lat": lat + 1, "lon": lon})

    def to_south(turn):
        return row_copy(turn, 1, 0, {"lat": lat - 1, "lon": lon})

    def over_north():
        return row_copy(0, 1, rows - 1, {"lat": lat, "lon": across})

    def over_south():
        return row_copy(0, 0, 0, {"lat": lat, "lon": across})

    @pl.when(last)
    def _():
        over_north().start()

    @pl.when(first)
    def _():
        over_south().start()

    @pl.when(jnp.logical_not(jnp.logical_or(last, border_south)))
    def _():
        to_north(0).start()

    @pl.when(jnp.logical_not(jnp.logical_or(first, border_north)))
    def _():
        to_south(0).start()

    def report(there):
        pl.semaphore_signal(
            ready, inc=1, device_id={"lat": there, "lon": lon}, device_id_type=MESH)

    @pl.when(beyond_south)
    def _():
        report(lat - 1)

    @pl.when(beyond_north)
    def _():
        report(lat + 1)

    @pl.when(polar)
    def _():
        for load in [cut_in] + tables_in[1:]:
            load.start()

    def rows_arrive(turn):
        @pl.when(jnp.logical_not(last))
        def _():
            to_south(turn).wait_recv()

        @pl.when(jnp.logical_not(first))
        def _():
            to_north(turn).wait_recv()

    def rows_left(turn):
        @pl.when(jnp.logical_not(last))
        def _():
            to_north(turn).wait_send()

        @pl.when(jnp.logical_not(first))
        def _():
            to_south(turn).wait_send()

    def poles_left():
        @pl.when(last)
        def _():
            over_north().wait_send()

        @pl.when(first)
        def _():
            over_south().wait_send()

    def poles_arrive():
        @pl.when(last)
        def _():
            over_north().wait_recv()

        @pl.when(first)
        def _():
            over_south().wait_recv()

    lane = lax.broadcasted_iota(jnp.int32, (levels, LANES), 1)
    end_tile = (cols - 1) // LANES * LANES
    end_lane = (cols - 1) % LANES
    east_tile = cols // LANES * LANES
    west_tile = width - LANES

    def pack_cols(turn):
        packed = jnp.zeros((levels, LANES), F32)

        def put(packed, at, tile, came_from):
            return jnp.where(lane == at, pltpu.roll(tile, (at - came_from) % LANES, 1), packed)

        for row in range(rows):
            packed = put(packed, row, q[row, :, end_tile:end_tile + LANES], end_lane)
            packed = put(packed, rows + row, q[row, :, 0:LANES], 0)
        return packed

    def pack_factors(packed):
        for row in range(rows):
            tile = zc[row, :, end_tile:cols]
            if cols - end_tile < LANES:
                tile = jnp.concatenate(
                    [tile, jnp.zeros((levels, LANES - cols + end_tile), F32)], axis=1)
            factor = DIFFUSION - 0.5 * tile
            packed = jnp.where(
                lane == 2 * rows + row,
                pltpu.roll(factor, (2 * rows + row - end_lane) % LANES, 1), packed)
            factor = DIFFUSION + 0.5 * zc[row, :, 0:LANES]
            packed = jnp.where(
                lane == 3 * rows + row, pltpu.roll(factor, 3 * rows + row, 1), packed)
        return packed

    def place_cols(turn):
        from_west = col_in[turn, lon_count - 1]
        from_east = col_in[turn, 1]
        for row in range(rows):
            tile = q[row, :, east_tile:east_tile + LANES]
            moved = pltpu.roll(from_east, (cols % LANES - rows - row) % LANES, 1)
            q[row, :, east_tile:east_tile + LANES] = jnp.where(lane == cols % LANES, moved, tile)
            tile = q[row, :, west_tile:west_tile + LANES]
            moved = pltpu.roll(from_west, (LANES - 1 - row) % LANES, 1)
            q[row, :, west_tile:west_tile + LANES] = jnp.where(lane == LANES - 1, moved, tile)

    def col_copy(turn, step):
        return pltpu.make_async_remote_copy(
            col_out.at[turn], col_in.at[turn, lon_count - step],
            col_send.at[turn, step], col_recv.at[turn, lon_count - step],
            device_id={"lat": lat, "lon": peers[step]}, device_id_type=MESH)

    def col_arrival(turn, step):
        theirs = col_in.at[turn, step]
        return pltpu.make_async_remote_copy(
            theirs, theirs, col_send.at[turn, step], col_recv.at[turn, step],
            device_id={"lat": lat, "lon": peers[step]}, device_id_type=MESH)

    def sum_copy(turn, piece, step):
        low, high = spans[turn][piece]
        return pltpu.make_async_remote_copy(
            part.at[turn, 0, low:high], part.at[turn, lon_count - step, low:high],
            sum_send.at[turn, piece, step], sum_recv.at[turn, piece, lon_count - step],
            device_id={"lat": lat, "lon": peers[step]}, device_id_type=MESH)

    def sum_arrival(turn, piece, step):
        low, high = spans[turn][piece]
        theirs = part.at[turn, step, low:high]
        return pltpu.make_async_remote_copy(
            theirs, theirs, sum_send.at[turn, piece, step], sum_recv.at[turn, piece, step],
            device_id={"lat": lat, "lon": peers[step]}, device_id_type=MESH)

    def farthest_first(send):
        for distance in range(lon_count - 1, 0, -1):
            @pl.when(lon + distance < lon_count)
            def _():
                send(distance)

            @pl.when(lon - distance >= 0)
            def _():
                send(lon_count - distance)

    def stencil(turn, row):
        beyond = row_first if turn == 0 else row_second
        here = q[row]
        to_east = pltpu.roll(here, width - 1, 1)[:, :cols]
        to_west = pltpu.roll(here, 1, 1)[:, :cols]
        here = here[:, :cols]
        up = q[row + 1, :, :cols] if row < rows - 1 else beyond[1, :, :cols]
        down = q[row - 1, :, :cols] if row else beyond[0, :, :cols]
        return (-0.5 * zc[row] * (to_east - to_west)
                - 0.5 * nc[row] * (up - down)
                + DIFFUSION * (to_east + to_west + up + down - 4.0 * here))

    q[:, :, (width - LANES):] = jnp.zeros((rows, levels, LANES), F32)
    for load in loads[:rows]:
        load.wait()
    for row in range(rows):
        q[row, :, :cols] = q_in[row]

    @pl.when(jnp.logical_not(polar))
    def _():
        col_out[0] = pack_cols(0)
        for side in (1, lon_count - 1):
            col_copy(0, side).start()
        for load in loads[rows:]:
            load.wait()
        for side in (1, lon_count - 1):
            col_arrival(0, side).wait_recv()
        place_cols(0)
        for row in range(1, rows - 1):
            tend[row, :, :cols] = stencil(0, row)

        def advance_edge(row):
            if row:
                to_south(0).wait_recv()
            else:
                to_north(0).wait_recv()
            q[row, :, :cols] = q[row, :, :cols] + stencil(0, row)
            if row:
                to_north(1).start()
            else:
                to_south(1).start()

        @pl.when(southern)
        def _():
            advance_edge(0)

            @pl.when(border_south)
            def _():
                pl.semaphore_wait(ready, 1)
                to_north(0).start()

            advance_edge(rows - 1)

        @pl.when(jnp.logical_not(southern))
        def _():
            advance_edge(rows - 1)

            @pl.when(border_north)
            def _():
                pl.semaphore_wait(ready, 1)
                to_south(0).start()

            advance_edge(0)

        for row in range(1, rows - 1):
            q[row, :, :cols] = q[row, :, :cols] + tend[row, :, :cols]
        col_out[1] = pack_cols(1)
        for side in (1, lon_count - 1):
            col_copy(1, side).start()
        for side in (1, lon_count - 1):
            col_arrival(1, side).wait_recv()
        rows_left(1)
        place_cols(1)
        for row in range(1, rows - 1):
            out[:, row, :] = q[row, :, :cols] + stencil(1, row)
        rows_arrive(1)
        for row in (0, rows - 1):
            out[:, row, :] = q[row, :, :cols] + stencil(1, row)
        rows_left(0)
        for turn in range(2):
            for side in (1, lon_count - 1):
                col_copy(turn, side).wait_send()

    @pl.when(polar)
    def _():
        tend[:, :, (width - LANES):] = jnp.zeros((rows, levels, LANES), F32)
        for load in loads[rows:2 * rows]:
            load.wait()
        col_out[0] = pack_factors(pack_cols(0))
        farthest_first(lambda step: col_copy(0, step).start())
        for load in loads[2 * rows:] + tables_in[:1]:
            load.wait()

        def analyse(turn, piece):
            low, high = pieces[turn][piece]
            count = high - low
            for slot in range(low, high):
                tend[slot, :, :cols] = stencil(turn, order[slot])
            found = dot_pair(tend[low:high].reshape(count * levels, width), ana)
            tiles = pack([found[row * levels:(row + 1) * levels] for row in range(count)], lane)
            for place, tile in enumerate(tiles):
                part[turn, 0, spans[turn][piece][0] + place] = tile
            farthest_first(lambda step: sum_copy(turn, piece, step).start())

        def collect(turn, piece):
            low, high = pieces[turn][piece]
            for step in steps:
                sum_arrival(turn, piece, step).wait_recv()
            count = high - low
            first_tile, end_tile_at = spans[turn][piece]
            gathered = jnp.concatenate(
                [jnp.concatenate(
                    unpack([part[turn, step, place] for place in range(first_tile, end_tile_at)],
                           count, lane), axis=0)
                 for step in range(lon_count)], axis=1)
            summed = dot3(gathered, exp).reshape(count, levels, 2 * KMAX)
            result = []
            for slot in range(low, high):
                total_sum = summed[slot - low]
                if turn == 0:
                    total_sum = total_sum + extra[slot]
                result.append(total_sum * keep[order[slot]])
            return result

        def synthesise(parts):
            return dot3(jnp.concatenate(parts, axis=0), syn).reshape(len(parts), levels, width)

        analyse(0, 0)
        rows_arrive(0)
        poles_arrive()
        analyse(0, 1)

        for load in tables_in[1:] + [cut_in]:
            load.wait()
        offset = jnp.where(
            lat < cap_blocks, lat * rows, (lat - lat_count + 2 * cap_blocks) * rows)
        mode = lax.broadcasted_iota(jnp.int32, (1, 2 * KMAX), 1) % KMAX
        weight = jnp.where(mode == 0, 1.0 / total, 2.0 / total).astype(F32)
        keep = [jnp.where(mode < cut_ref[offset + row], weight, 0.0) for row in range(rows)]
        parity = 1.0 - 2.0 * (lax.broadcasted_iota(jnp.int32, (1, 2 * KMAX), 1) % 2).astype(F32)

        for step in steps:
            col_arrival(0, step).wait_recv()
        col_in[0, 0] = col_out[0]
        place_cols(0)
        packed = [col_in[0, step] for step in range(lon_count)]
        added = [jnp.zeros((levels, 2 * KMAX), F32) for _ in range(rows)]
        for step in range(lon_count):
            behind = packed[step - 1]
            ahead = packed[(step + 1) % lon_count]
            at_last = packed[step] * pltpu.roll(ahead, rows, 1)
            at_first = packed[step] * pltpu.roll(behind, 3 * rows, 1)
            for row in range(rows):
                column = at_last[:, 2 * rows + row:2 * rows + row + 1]
                added[row] = added[row] + column * ends[step, 1:2, :]
                column = at_first[:, 3 * rows + row:3 * rows + row + 1]
                added[row] = added[row] + column * ends[step, 0:1, :]
        for slot in range(rows):
            extra[slot] = added[order[slot]]

        low, high = pieces[0][0]
        filtered = synthesise(collect(0, 0))
        for slot in range(low, high):
            q[order[slot]] = q[order[slot]] + filtered[slot - low]
        analyse(1, 0)

        local = collect(0, 1)
        pole_row = jnp.where(first, local[0], local[1]) * parity
        filtered = synthesise(local + [pole_row])
        q[0] = q[0] + filtered[0]
        q[rows - 1] = q[rows - 1] + filtered[1]

        @pl.when(jnp.logical_not(last))
        def _():
            to_north(1).start()

        @pl.when(jnp.logical_not(first))
        def _():
            to_south(1).start()

        @pl.when(last)
        def _():
            row_second[1, :, :cols] = row_first[1] + filtered[2, :, :cols]

        @pl.when(first)
        def _():
            row_second[0, :, :cols] = row_first[0] + filtered[2, :, :cols]

        rows_arrive(1)
        analyse(1, 1)
        for piece in range(2):
            low, high = pieces[1][piece]
            filtered = synthesise(collect(1, piece))
            for slot in range(low, high):
                row = order[slot]
                out[:, row, :] = q[row, :, :cols] + filtered[slot - low, :, :cols]
        rows_left(0)
        rows_left(1)
        poles_left()
        for step in steps:
            col_copy(0, step).wait_send()
            for turn in range(2):
                for piece in range(2):
                    sum_copy(turn, piece, step).wait_send()


def shards(tracer, zonal_courant, north_courant, cutoff):
    levels, rows, cols = tracer.shape
    lat_count = lax.axis_size("lat")
    lon_count = lax.axis_size("lon")
    cap_blocks = lat_count // 8
    width = -(-(cols + 2) // LANES) * LANES
    analysis, expand, synthesis, ends = tables(cols, width, lon_count)
    dma = pltpu.SemaphoreType.DMA
    anywhere = pl.BlockSpec(memory_space=pl.ANY)
    return pl.pallas_call(
        functools.partial(kernel, lat_count, lon_count, cap_blocks),
        out_shape=pltpu.VMEM(tracer.shape, F32),
        in_specs=[anywhere] * 8,
        out_specs=pl.BlockSpec(memory_space=pltpu.VMEM),
        scratch_shapes=[
            pltpu.SMEM(cutoff.shape, jnp.int32),
            pltpu.VMEM((rows, levels, cols), F32),
            pltpu.VMEM((rows, levels, cols), F32),
            pltpu.VMEM((rows, levels, cols), F32),
            pltpu.VMEM(analysis.shape, BF16),
            pltpu.VMEM(expand.shape, BF16),
            pltpu.VMEM(synthesis.shape, BF16),
            pltpu.VMEM(ends.shape, F32),
            pltpu.VMEM((rows, levels, width), F32),
            pltpu.VMEM((rows, levels, width), F32),
            pltpu.VMEM((2, levels, cols), F32),
            pltpu.VMEM((2, levels, width), F32),
            pltpu.VMEM((2, levels, LANES), F32),
            pltpu.VMEM((2, lon_count, levels, LANES), F32),
            pltpu.VMEM((2, lon_count, rows, levels, LANES), F32),
            pltpu.VMEM((rows, levels, 2 * KMAX), F32),
            dma((3 * rows + 5,)), pltpu.SemaphoreType.REGULAR,
            dma((2, 2)), dma((2, 2)), dma((2, lon_count)), dma((2, lon_count)),
            dma((2, 2, lon_count)), dma((2, 2, lon_count)),
        ],
        compiler_params=pltpu.CompilerParams(collective_id=0, has_side_effects=True),
    )(cutoff, tracer, zonal_courant, north_courant,
      jnp.asarray(analysis), jnp.asarray(expand), jnp.asarray(synthesis), jnp.asarray(ends))


def solution(mesh):
    return jax.shard_map(
        shards,
        mesh=mesh,
        in_specs=(P(None, "lat", "lon"), P(None, "lat", "lon"), P(None, "lat", "lon"), P()),
        out_specs=P(None, "lat", "lon"),
        check_vma=False,
    )
```

```python
import functools
import math

import jax
import jax.numpy as jnp
import numpy as np
from jax import lax
from jax.experimental import pallas as pl
from jax.experimental.pallas import tpu as pltpu
from jax.sharding import PartitionSpec as P

KMAX = 128
DIFFUSION = 0.2
LANES = 128
QUARTER = LANES // 4
KEPT = 3 * QUARTER
MESH = pl.DeviceIdType.MESH
F32 = jnp.float32
BF16 = jnp.bfloat16


def split_table(table):
    high = table.astype(np.float32).astype(BF16)
    low = (table - high.astype(np.float64)).astype(np.float32).astype(BF16)
    return np.stack([high, low])


def trig(columns, total):
    modes = np.arange(KMAX)
    angle = (columns[:, None] * modes[None, :] % total) * (2.0 * math.pi / total)
    return np.concatenate([np.cos(angle), np.sin(angle)], axis=1)


def window_basis(cols, total):
    bandwidth = (KMAX - 0.5) / total
    place = np.arange(cols)
    operator = np.diag(((cols - 1 - 2 * place) / 2.0) ** 2 * math.cos(2.0 * math.pi * bandwidth))
    beside = np.arange(1, cols) * (cols - np.arange(1, cols)) / 2.0
    operator = operator + np.diag(beside, 1) + np.diag(beside, -1)
    vectors = np.linalg.eigh(operator)[1][:, ::-1]
    half = vectors[:(cols + 1) // 2]
    peak = np.take_along_axis(half, np.abs(half).argmax(0)[None], 0)[0]
    return vectors * np.where(peak < 0, -1.0, 1.0)


def tables(cols, width, lon_count):
    total = cols * lon_count
    basis = np.zeros((width, LANES))
    basis[:cols, :KEPT] = window_basis(cols, total)[:, :KEPT]
    waves = trig(np.arange(cols), total)
    assert np.abs(waves - basis[:cols] @ (basis[:cols].T @ waves)).max() < 1e-11
    analysis = np.concatenate(list(split_table(basis)), axis=1)
    expand = np.zeros((lon_count, LANES, 2 * KMAX))
    for step in range(lon_count):
        expand[step] = basis[:cols].T @ trig(np.arange(cols) + step * cols, total)
    expand = split_table(expand.reshape(lon_count * LANES, 2 * KMAX))
    lane = np.arange(width)
    lane = np.where(lane == width - 1, -1, lane)
    synthesis = split_table(trig(lane, total).T.copy())
    ends = np.zeros((lon_count, 8, 2 * KMAX), np.float32)
    ends[:, 0] = trig(np.arange(lon_count) * cols, total)
    ends[:, 1] = trig(np.arange(lon_count) * cols + cols - 1, total)
    return analysis, expand, synthesis, ends


def split(value):
    high = value.astype(BF16)
    low = (value - high.astype(F32)).astype(BF16)
    return high, low


def dot3(value, table):
    high, low = split(value)
    t_high = table[0]
    t_low = table[1]
    dot = functools.partial(jnp.dot, preferred_element_type=F32)
    return dot(high, t_high) + (dot(low, t_high) + dot(high, t_low))


def dot_pair(value, table):
    size = value.shape[0]
    both = jnp.dot(jnp.concatenate(split(value), axis=0), table[...], preferred_element_type=F32)
    return both[:size, :LANES] + (both[:size, LANES:] + both[size:, :LANES])


def packed_tiles(count):
    return count // 4 * 3 + count % 4


def pack(values, lane):
    tiles = []
    while len(values) >= 4:
        fourth = values[3]
        for place in range(3):
            moved = pltpu.roll(fourth, KEPT - place * QUARTER, 1)
            tiles.append(jnp.where(lane >= KEPT, moved, values[place]))
        values = values[4:]
    return tiles + values


def unpack(tiles, count, lane):
    values = []
    while count >= 4:
        moved = [pltpu.roll(tiles[place], (place + 1) * QUARTER, 1) for place in range(3)]
        fourth = jnp.where(
            lane < QUARTER, moved[0], jnp.where(lane < 2 * QUARTER, moved[1], moved[2]))
        values += tiles[:3] + [fourth]
        tiles = tiles[3:]
        count -= 4
    return values + tiles


def kernel(
    lat_count, lon_count, cap_blocks,
    cut_hbm, tracer, zonal, north, ana_hbm, exp_hbm, syn_hbm, ends_hbm, out,
    cut_ref, q_in, zc, nc, ana, exp, syn, ends, q, tend,
    row_first, row_second, col_out, col_in, part, extra,
    load_sem, ready, row_send, row_recv, col_send, col_recv, sum_send, sum_recv,
):
    rows, levels, cols = q_in.shape
    width = q.shape[2]
    total = cols * lon_count
    lat = lax.axis_index("lat")
    lon = lax.axis_index("lon")
    polar = jnp.logical_or(lat < cap_blocks, lat >= lat_count - cap_blocks)
    first = lat == 0
    last = lat == lat_count - 1
    southern = 2 * lat < lat_count
    border_south = lat == cap_blocks
    border_north = lat == lat_count - 1 - cap_blocks
    beyond_south = lat == cap_blocks + 1
    beyond_north = lat == lat_count - 2 - cap_blocks
    east = lax.rem(lon + 1, lon_count)
    west = lax.rem(lon + lon_count - 1, lon_count)
    across = lax.rem(lon + lon_count // 2, lon_count)
    peers = [lax.rem(lon + step, lon_count) for step in range(lon_count)]
    steps = range(1, lon_count)
    order = [0, rows - 1, 1, rows - 2] + list(range(2, rows - 2))
    pieces = (((2, rows), (0, 2)), ((4, rows), (0, 4)))
    spans = [[], []]
    for turn in range(2):
        used = 0
        for low, high in pieces[turn]:
            spans[turn].append((used, used + packed_tiles(high - low)))
            used = spans[turn][-1][1]

    loads = []
    for index, (source, target) in enumerate(((tracer, q_in), (zonal, zc), (north, nc))):
        for row in range(rows):
            loads.append(pltpu.make_async_copy(
                source.at[:, row, :], target.at[row],
                load_sem.at[index * rows + row]))
    cut_in = pltpu.make_async_copy(cut_hbm, cut_ref, load_sem.at[3 * rows + 4])

    barrier = pltpu.get_barrier_semaphore()

    def greet(there):
        pl.semaphore_signal(barrier, inc=1, device_id=there, device_id_type=MESH)

    @pl.when(jnp.logical_not(jnp.logical_or(first, beyond_south)))
    def _():
        greet({"lat": lat - 1, "lon": lon})

    @pl.when(jnp.logical_not(jnp.logical_or(last, beyond_north)))
    def _():
        greet({"lat": lat + 1, "lon": lon})

    @pl.when(polar)
    def _():
        for step in steps:
            greet({"lat": lat, "lon": peers[step]})

    @pl.when(jnp.logical_not(polar))
    def _():
        greet({"lat": lat, "lon": east})
        greet({"lat": lat, "lon": west})

    tables_in = [
        pltpu.make_async_copy(ana_hbm, ana, load_sem.at[3 * rows]),
        pltpu.make_async_copy(exp_hbm, exp, load_sem.at[3 * rows + 1]),
        pltpu.make_async_copy(syn_hbm, syn, load_sem.at[3 * rows + 2]),
        pltpu.make_async_copy(ends_hbm, ends, load_sem.at[3 * rows + 3]),
    ]
    for load in loads[:2 * rows]:
        load.start()

    @pl.when(polar)
    def _():
        tables_in[0].start()

    for load in loads[2 * rows:]:
        load.start()

    edge = jnp.logical_or(
        jnp.logical_or(first, last), jnp.logical_or(border_south, border_north)).astype(jnp.int32)
    sides = jnp.where(polar, lon_count - 1, 2)
    early = jnp.logical_and(polar, 2 * lon < lon_count)
    late = jnp.logical_not(early)

    def meet():
        pl.semaphore_wait(barrier, 2 - edge + sides)

    def row_copy(turn, slot, row, there):
        source = tracer.at[:, row, :] if turn == 0 else q.at[row]
        target = row_first if turn == 0 else row_second
        return pltpu.make_async_remote_copy(
            source, target.at[slot],
            row_send.at[turn, 0 if row else 1], row_recv.at[turn, slot],
            device_id=there, device_id_type=MESH)

    def to_north(turn):
        return row_copy(turn, 0, rows - 1, {"lat": lat + 1, "lon": lon})

    def to_south(turn):
        return row_copy(turn, 1, 0, {"lat": lat - 1, "lon": lon})

    def over_north():
        return row_copy(0, 1, rows - 1, {"lat": lat, "lon": across})

    def over_south():
        return row_copy(0, 0, 0, {"lat": lat, "lon": across})

    def exchange_rows():
        @pl.when(last)
        def _():
            over_north().start()

        @pl.when(first)
        def _():
            over_south().start()

        @pl.when(jnp.logical_not(jnp.logical_or(last, border_south)))
        def _():
            to_north(0).start()

        @pl.when(jnp.logical_not(jnp.logical_or(first, border_north)))
        def _():
            to_south(0).start()

    @pl.when(late)
    def _():
        meet()
        exchange_rows()

    def report(there):
        pl.semaphore_signal(
            ready, inc=1, device_id={"lat": there, "lon": lon}, device_id_type=MESH)

    @pl.when(beyond_south)
    def _():
        report(lat - 1)

    @pl.when(beyond_north)
    def _():
        report(lat + 1)

    @pl.when(polar)
    def _():
        for load in [cut_in] + tables_in[1:]:
            load.start()

    def rows_arrive(turn):
        @pl.when(jnp.logical_not(last))
        def _():
            to_south(turn).wait_recv()

        @pl.when(jnp.logical_not(first))
        def _():
            to_north(turn).wait_recv()

    def rows_left(turn):
        @pl.when(jnp.logical_not(last))
        def _():
            to_north(turn).wait_send()

        @pl.when(jnp.logical_not(first))
        def _():
            to_south(turn).wait_send()

    def poles_left():
        @pl.when(last)
        def _():
            over_north().wait_send()

        @pl.when(first)
        def _():
            over_south().wait_send()

    def poles_arrive():
        @pl.when(last)
        def _():
            over_north().wait_recv()

        @pl.when(first)
        def _():
            over_south().wait_recv()

    lane = lax.broadcasted_iota(jnp.int32, (levels, LANES), 1)
    end_tile = (cols - 1) // LANES * LANES
    end_lane = (cols - 1) % LANES
    east_tile = cols // LANES * LANES
    west_tile = width - LANES

    def pack_cols(turn):
        packed = jnp.zeros((levels, LANES), F32)

        def put(packed, at, tile, came_from):
            return jnp.where(lane == at, pltpu.roll(tile, (at - came_from) % LANES, 1), packed)

        for row in range(rows):
            packed = put(packed, row, q[row, :, end_tile:end_tile + LANES], end_lane)
            packed = put(packed, rows + row, q[row, :, 0:LANES], 0)
        return packed

    def pack_factors(packed):
        for row in range(rows):
            tile = zc[row, :, end_tile:cols]
            if cols - end_tile < LANES:
                tile = jnp.concatenate(
                    [tile, jnp.zeros((levels, LANES - cols + end_tile), F32)], axis=1)
            factor = DIFFUSION - 0.5 * tile
            packed = jnp.where(
                lane == 2 * rows + row,
                pltpu.roll(factor, (2 * rows + row - end_lane) % LANES, 1), packed)
            factor = DIFFUSION + 0.5 * zc[row, :, 0:LANES]
            packed = jnp.where(
                lane == 3 * rows + row, pltpu.roll(factor, 3 * rows + row, 1), packed)
        return packed

    def place_cols(turn):
        from_west = col_in[turn, lon_count - 1]
        from_east = col_in[turn, 1]
        for row in range(rows):
            tile = q[row, :, east_tile:east_tile + LANES]
            moved = pltpu.roll(from_east, (cols % LANES - rows - row) % LANES, 1)
            q[row, :, east_tile:east_tile + LANES] = jnp.where(lane == cols % LANES, moved, tile)
            tile = q[row, :, west_tile:west_tile + LANES]
            moved = pltpu.roll(from_west, (LANES - 1 - row) % LANES, 1)
            q[row, :, west_tile:west_tile + LANES] = jnp.where(lane == LANES - 1, moved, tile)

    def col_copy(turn, step):
        return pltpu.make_async_remote_copy(
            col_out.at[turn], col_in.at[turn, lon_count - step],
            col_send.at[turn, step], col_recv.at[turn, lon_count - step],
            device_id={"lat": lat, "lon": peers[step]}, device_id_type=MESH)

    def col_arrival(turn, step):
        theirs = col_in.at[turn, step]
        return pltpu.make_async_remote_copy(
            theirs, theirs, col_send.at[turn, step], col_recv.at[turn, step],
            device_id={"lat": lat, "lon": peers[step]}, device_id_type=MESH)

    def sum_copy(turn, piece, step):
        low, high = spans[turn][piece]
        return pltpu.make_async_remote_copy(
            part.at[turn, 0, low:high], part.at[turn, lon_count - step, low:high],
            sum_send.at[turn, piece, step], sum_recv.at[turn, piece, lon_count - step],
            device_id={"lat": lat, "lon": peers[step]}, device_id_type=MESH)

    def sum_arrival(turn, piece, step):
        low, high = spans[turn][piece]
        theirs = part.at[turn, step, low:high]
        return pltpu.make_async_remote_copy(
            theirs, theirs, sum_send.at[turn, piece, step], sum_recv.at[turn, piece, step],
            device_id={"lat": lat, "lon": peers[step]}, device_id_type=MESH)

    def farthest_first(send):
        for distance in range(lon_count - 1, 0, -1):
            @pl.when(lon + distance < lon_count)
            def _():
                send(distance)

            @pl.when(lon - distance >= 0)
            def _():
                send(lon_count - distance)

    def stencil(turn, row):
        beyond = row_first if turn == 0 else row_second
        here = q[row]
        to_east = pltpu.roll(here, width - 1, 1)[:, :cols]
        to_west = pltpu.roll(here, 1, 1)[:, :cols]
        here = here[:, :cols]
        up = q[row + 1, :, :cols] if row < rows - 1 else beyond[1, :, :cols]
        down = q[row - 1, :, :cols] if row else beyond[0, :, :cols]
        return (-0.5 * zc[row] * (to_east - to_west)
                - 0.5 * nc[row] * (up - down)
                + DIFFUSION * (to_east + to_west + up + down - 4.0 * here))

    q[:, :, (width - LANES):] = jnp.zeros((rows, levels, LANES), F32)
    for load in loads[:rows]:
        load.wait()
    for row in range(rows):
        q[row, :, :cols] = q_in[row]

    @pl.when(jnp.logical_not(polar))
    def _():
        col_out[0] = pack_cols(0)
        for side in (1, lon_count - 1):
            col_copy(0, side).start()
        for load in loads[rows:]:
            load.wait()
        for side in (1, lon_count - 1):
            col_arrival(0, side).wait_recv()
        place_cols(0)
        for row in range(1, rows - 1):
            tend[row, :, :cols] = stencil(0, row)

        def advance_edge(row):
            if row:
                to_south(0).wait_recv()
            else:
                to_north(0).wait_recv()
            q[row, :, :cols] = q[row, :, :cols] + stencil(0, row)
            if row:
                to_north(1).start()
            else:
                to_south(1).start()

        @pl.when(southern)
        def _():
            advance_edge(0)

            @pl.when(border_south)
            def _():
                pl.semaphore_wait(ready, 1)
                to_north(0).start()

            advance_edge(rows - 1)

        @pl.when(jnp.logical_not(southern))
        def _():
            advance_edge(rows - 1)

            @pl.when(border_north)
            def _():
                pl.semaphore_wait(ready, 1)
                to_south(0).start()

            advance_edge(0)

        for row in range(1, rows - 1):
            q[row, :, :cols] = q[row, :, :cols] + tend[row, :, :cols]
        col_out[1] = pack_cols(1)
        for side in (1, lon_count - 1):
            col_copy(1, side).start()
        for side in (1, lon_count - 1):
            col_arrival(1, side).wait_recv()
        rows_left(1)
        place_cols(1)
        for row in range(1, rows - 1):
            out[:, row, :] = q[row, :, :cols] + stencil(1, row)
        rows_arrive(1)
        for row in (0, rows - 1):
            out[:, row, :] = q[row, :, :cols] + stencil(1, row)
        rows_left(0)
        for turn in range(2):
            for side in (1, lon_count - 1):
                col_copy(turn, side).wait_send()

    @pl.when(polar)
    def _():
        tend[:, :, (width - LANES):] = jnp.zeros((rows, levels, LANES), F32)
        for load in loads[rows:2 * rows]:
            load.wait()
        col_out[0] = pack_factors(pack_cols(0))

        @pl.when(late)
        def _():
            farthest_first(lambda step: col_copy(0, step).start())

        for load in loads[2 * rows:] + tables_in[:1]:
            load.wait()

        def analyse(turn, piece):
            low, high = pieces[turn][piece]
            count = high - low
            for slot in range(low, high):
                tend[slot, :, :cols] = stencil(turn, order[slot])
            found = dot_pair(tend[low:high].reshape(count * levels, width), ana)
            tiles = pack([found[row * levels:(row + 1) * levels] for row in range(count)], lane)
            for place, tile in enumerate(tiles):
                part[turn, 0, spans[turn][piece][0] + place] = tile

        def share(turn, piece):
            farthest_first(lambda step: sum_copy(turn, piece, step).start())

        def collect(turn, piece):
            low, high = pieces[turn][piece]
            for step in steps:
                sum_arrival(turn, piece, step).wait_recv()
            count = high - low
            first_tile, end_tile_at = spans[turn][piece]
            gathered = jnp.concatenate(
                [jnp.concatenate(
                    unpack([part[turn, step, place] for place in range(first_tile, end_tile_at)],
                           count, lane), axis=0)
                 for step in range(lon_count)], axis=1)
            summed = dot3(gathered, exp).reshape(count, levels, 2 * KMAX)
            result = []
            for slot in range(low, high):
                total_sum = summed[slot - low]
                if turn == 0:
                    total_sum = total_sum + extra[slot]
                result.append(total_sum * keep[order[slot]])
            return result

        def synthesise(parts):
            return dot3(jnp.concatenate(parts, axis=0), syn).reshape(len(parts), levels, width)

        analyse(0, 0)

        @pl.when(early)
        def _():
            meet()
            exchange_rows()
            farthest_first(lambda step: col_copy(0, step).start())

        share(0, 0)
        rows_arrive(0)
        poles_arrive()
        analyse(0, 1)
        share(0, 1)

        for load in tables_in[1:] + [cut_in]:
            load.wait()
        offset = jnp.where(
            lat < cap_blocks, lat * rows, (lat - lat_count + 2 * cap_blocks) * rows)
        mode = lax.broadcasted_iota(jnp.int32, (1, 2 * KMAX), 1) % KMAX
        weight = jnp.where(mode == 0, 1.0 / total, 2.0 / total).astype(F32)
        keep = [jnp.where(mode < cut_ref[offset + row], weight, 0.0) for row in range(rows)]
        parity = 1.0 - 2.0 * (lax.broadcasted_iota(jnp.int32, (1, 2 * KMAX), 1) % 2).astype(F32)

        for step in steps:
            col_arrival(0, step).wait_recv()
        col_in[0, 0] = col_out[0]
        place_cols(0)
        packed = [col_in[0, step] for step in range(lon_count)]
        added = [jnp.zeros((levels, 2 * KMAX), F32) for _ in range(rows)]
        for step in range(lon_count):
            behind = packed[step - 1]
            ahead = packed[(step + 1) % lon_count]
            at_last = packed[step] * pltpu.roll(ahead, rows, 1)
            at_first = packed[step] * pltpu.roll(behind, 3 * rows, 1)
            for row in range(rows):
                column = at_last[:, 2 * rows + row:2 * rows + row + 1]
                added[row] = added[row] + column * ends[step, 1:2, :]
                column = at_first[:, 3 * rows + row:3 * rows + row + 1]
                added[row] = added[row] + column * ends[step, 0:1, :]
        for slot in range(rows):
            extra[slot] = added[order[slot]]

        low, high = pieces[0][0]
        filtered = synthesise(collect(0, 0))
        for slot in range(low, high):
            q[order[slot]] = q[order[slot]] + filtered[slot - low]
        analyse(1, 0)
        share(1, 0)

        local = collect(0, 1)
        pole_row = jnp.where(first, local[0], local[1]) * parity
        filtered = synthesise(local + [pole_row])
        q[0] = q[0] + filtered[0]
        q[rows - 1] = q[rows - 1] + filtered[1]

        @pl.when(jnp.logical_not(last))
        def _():
            to_north(1).start()

        @pl.when(jnp.logical_not(first))
        def _():
            to_south(1).start()

        @pl.when(last)
        def _():
            row_second[1, :, :cols] = row_first[1] + filtered[2, :, :cols]

        @pl.when(first)
        def _():
            row_second[0, :, :cols] = row_first[0] + filtered[2, :, :cols]

        rows_arrive(1)
        analyse(1, 1)
        share(1, 1)
        for piece in range(2):
            low, high = pieces[1][piece]
            filtered = synthesise(collect(1, piece))
            for slot in range(low, high):
                row = order[slot]
                out[:, row, :] = q[row, :, :cols] + filtered[slot - low, :, :cols]
        rows_left(0)
        rows_left(1)
        poles_left()
        for step in steps:
            col_copy(0, step).wait_send()
            for turn in range(2):
                for piece in range(2):
                    sum_copy(turn, piece, step).wait_send()


def shards(tracer, zonal_courant, north_courant, cutoff):
    levels, rows, cols = tracer.shape
    lat_count = lax.axis_size("lat")
    lon_count = lax.axis_size("lon")
    cap_blocks = lat_count // 8
    width = -(-(cols + 2) // LANES) * LANES
    analysis, expand, synthesis, ends = tables(cols, width, lon_count)
    dma = pltpu.SemaphoreType.DMA
    anywhere = pl.BlockSpec(memory_space=pl.ANY)
    return pl.pallas_call(
        functools.partial(kernel, lat_count, lon_count, cap_blocks),
        out_shape=pltpu.VMEM(tracer.shape, F32),
        in_specs=[anywhere] * 8,
        out_specs=pl.BlockSpec(memory_space=pltpu.VMEM),
        scratch_shapes=[
            pltpu.SMEM(cutoff.shape, jnp.int32),
            pltpu.VMEM((rows, levels, cols), F32),
            pltpu.VMEM((rows, levels, cols), F32),
            pltpu.VMEM((rows, levels, cols), F32),
            pltpu.VMEM(analysis.shape, BF16),
            pltpu.VMEM(expand.shape, BF16),
            pltpu.VMEM(synthesis.shape, BF16),
            pltpu.VMEM(ends.shape, F32),
            pltpu.VMEM((rows, levels, width), F32),
            pltpu.VMEM((rows, levels, width), F32),
            pltpu.VMEM((2, levels, cols), F32),
            pltpu.VMEM((2, levels, width), F32),
            pltpu.VMEM((2, levels, LANES), F32),
            pltpu.VMEM((2, lon_count, levels, LANES), F32),
            pltpu.VMEM((2, lon_count, rows, levels, LANES), F32),
            pltpu.VMEM((rows, levels, 2 * KMAX), F32),
            dma((3 * rows + 5,)), pltpu.SemaphoreType.REGULAR,
            dma((2, 2)), dma((2, 2)), dma((2, lon_count)), dma((2, lon_count)),
            dma((2, 2, lon_count)), dma((2, 2, lon_count)),
        ],
        compiler_params=pltpu.CompilerParams(collective_id=0, has_side_effects=True),
    )(cutoff, tracer, zonal_courant, north_courant,
      jnp.asarray(analysis), jnp.asarray(expand), jnp.asarray(synthesis), jnp.asarray(ends))


def solution(mesh):
    return jax.shard_map(
        shards,
        mesh=mesh,
        in_specs=(P(None, "lat", "lon"), P(None, "lat", "lon"), P(None, "lat", "lon"), P()),
        out_specs=P(None, "lat", "lon"),
        check_vma=False,
    )
```
